32 devices in a mesh: grp: 8 (over z, core), dev: 4 (over y, x).
Axes of the slice: x: 2, y: 2, z: 4, core: 2. Of those that a mesh axis runs over, the one named last changes fastest.
Arguments:
- orbitals: bfloat16 [64, 256, 1024], P(('grp', 'dev')), may hold values from -6 to 6
- dens_tiles: bfloat16 [1024, 128, 128], P(('grp', 'dev')), may hold values from -0.005859375 to 0.005859375
- point_coords: float32 [3, 16384], P(None, ('grp', 'dev')), may hold values from 0 to 64
- point_weights: float32 [16384], P(('grp', 'dev')), may hold values from 0.005 to 0.05
- batch_blocks: int32 [64, 8], P(('grp', 'dev')), may hold values from 0 to 8, all different within a row
- tile_owner: int32 [2592, 1], P(('grp', 'dev')), may hold values from 0 to 3; in each aligned block of 81 rows (0 to 80, 81 to 161, ...) at most 31 rows name the same one
- tile_slot: int32 [2592], P(('grp', 'dev')), may hold values from 0 to 31
- batch_atoms: int32 [64, 4], P(('grp', 'dev')), may hold values from 0 to 3, all different within a row
- batch_weights: int32 [64, 4], P(('grp', 'dev')), may hold values from 1 to 8
- atom_grid_index: int32 [3, 32], P(None, 'grp'), may hold values from 0 to 63
Outputs:
- density: float32 [16384], P(('grp', 'dev'))
- potential: float32 [16384], P(('grp', 'dev'))
- ham_tiles: bfloat16 [1024, 128, 128], P(('grp', 'dev'))
The draws below stay inside these ranges and needn't reach their ends.
Inputs may be any that keep to these rules, and one draw needn't show every extreme that they name: `tile_owner`: in each aligned block of 81 rows (the listed tiles of one device) no owner is named by more than 31 rows, a bound that some block reaches. `batch_blocks`: the 8 blocks of a batch are distinct. `batch_atoms`: the 4 atoms of a batch are distinct.
All inputs are finite; a program needn't handle non-finite values.
Results may differ from the reference program's by a relative error of at most 0.0056.
Values may be sent and summed in bfloat16 or wider, within the bound.
A program may use at most 64 MiB of HBM per device.

```python
import math
import jax
import jax.numpy as jnp
import numpy as np
from jax import lax

TB = 128
BB = 8
BORB = 1024
UB = 9
R = 81
PTS = 256
BAT_DEV = 2
KM = 512
NEAR = 4
TILE_DEV = 32
GRIDN = 64
OWNERS = 4
CAP = 31
ATOM_GRP = 4
ATOMS = 32
BATCHES = 64
POINTS = 16384
TILES = 1024
REQS = 2592
N_GRP = 8
N_DEV = 4


def with_ends(array, key, smallest, largest):
    longest = array.shape.index(max(array.shape))
    spots = []
    for shift in (0, 1):
        where = [jax.random.randint(jax.random.fold_in(key, axis), (), 0, length) for axis, length in enumerate(array.shape)]
        where[longest] = (where[longest] + shift) % array.shape[longest]
        spots.append(tuple(where))
    return array.at[spots[0]].set(smallest).at[spots[1]].set(largest)


def level_of(key, dims, split, smallest, high):
    gain, own = 1.0, jax.random.fold_in(key, 6)
    for axis_at, shards_of in split:
        draws = jnp.exp(jax.random.uniform(jax.random.fold_in(own, axis_at), (shards_of,), jnp.float32, smallest / len(split), high / len(split)))
        gain = gain * jnp.repeat(draws, dims[axis_at] // shards_of).reshape([-1 if axis == axis_at else 1 for axis in range(len(dims))])
    return gain


def different_ones(own_key, rows, count, top, lift):
    sequence = jax.random.permutation(jax.random.fold_in(own_key, 1), count)
    pull = sequence
    for power in range(3):
        pull = pull * pull // count
    pull = pull * lift // count
    lots = jax.random.randint(jax.random.fold_in(own_key, 2), (rows, count), 0, 4096) + pull
    holders = jax.random.permutation(jax.random.fold_in(own_key, 3), rows)[jnp.arange(count) % rows]
    lots = jnp.where(jnp.arange(rows)[:, None] == holders[None, :], 1 << 14, lots)
    merit = lots * count + jnp.arange(count)
    return lax.top_k(merit.astype(jnp.int32), top)[1].astype(jnp.int32)


def deal_out(stream_key, own, number, rows, amount, top, limit, lean):
    order = jax.random.permutation(stream_key, amount)
    packed, usual = shares(amount, rows * top, limit, lean, True), shares(amount, rows * top, limit, lean, False)
    places = jnp.arange(amount)

    def named(tallies, offset_by):
        used = int((tallies > 0).sum())
        fixed = max(1, used // 4)
        moved = fixed + (places - fixed + offset_by * (used - fixed)) % max(1, amount - fixed)
        return jnp.zeros((amount,), jnp.int32).at[order[jnp.where(places < fixed, places, moved)]].set(jnp.asarray(tallies, jnp.int32))

    tallies = jnp.where(number % 4 == 0, named(packed, number // 4), named(usual, number - number // 4 - 1))
    mixed = jax.random.permutation(jax.random.fold_in(own, 3), amount)
    donor, taker = mixed[0:amount // 2 * 2:2], mixed[1:amount // 2 * 2:2]
    margin = jnp.minimum(tallies[donor] - 1, limit - tallies[taker]) // 2
    margin = jnp.where((donor == order[0]) | (taker == order[0]) | (tallies[taker] == 0), 0, jnp.maximum(margin, 0))
    moved = jax.random.randint(jax.random.fold_in(own, 4), (amount // 2,), 0, 1 << 20) % (margin + 1)
    tallies = tallies.at[donor].add(-moved).at[taker].add(moved)
    items = jnp.searchsorted(jnp.cumsum(tallies), jnp.arange(rows * top), side="right").astype(jnp.int32)
    table = items.reshape(top, rows).T
    table = table[jax.random.permutation(jax.random.fold_in(own, 1), rows)]
    offset_by = jax.random.randint(jax.random.fold_in(own, 2), (rows, 1), 0, top)
    return jnp.take_along_axis(table, (jnp.arange(top)[None, :] + offset_by) % top, axis=1)


def shares(amount, total, bound, slope, full):
    portions = [(1 << 20) // math.isqrt(rank ** slope) + 1 for rank in range(1, amount + 1)]
    largest = bound if full else min(bound, max(-(-total // amount), total * portions[0] // sum(portions)))
    least = 1 if total - largest >= amount - 1 else 0
    holding, spare = [largest] + [least] * (amount - 1), total - largest - least * (amount - 1)
    while spare > 0:
        free = [i for i in range(1, amount) if holding[i] < largest] or [i for i in range(1, amount) if holding[i] < bound]
        whole, left = sum([portions[i] for i in free]), spare
        for i in free:
            more = min(bound - holding[i], max(1, left * portions[i] // whole), spare)
            holding[i] = holding[i] + more
            spare = spare - more
    return np.array(holding)


def gaussian(stream_key, dims, width, limit, split=(), kind=jnp.bfloat16):
    drawn = jax.random.normal(stream_key, dims, jnp.float32) * width
    if len(split) > 0:
        drawn = level_of(stream_key, dims, split, -0.22, 0.18) * drawn
    return jnp.clip(drawn, min=-limit, max=limit).astype(kind)


def setup_inputs(seed: int = 0) -> dict:
    streams_of = jax.random.split(jax.random.key(seed), 11)
    orbitals = gaussian(streams_of[0], (BATCHES, PTS, BORB), 1.0, 6.0, ((0, 32),))
    dens_tiles = gaussian(streams_of[1], (TILES, TB, TB), (1.0 / BORB), 0.005859375, ((0, 32),))
    point_coords = jnp.clip(64.0 * jax.random.uniform(streams_of[2], (3, POINTS), jnp.float32) ** level_of(streams_of[2], (3, POINTS), ((1, 32),), -0.2, 0.2), 0.0, 64.0)
    point_weights = jnp.clip(jnp.exp(math.log(0.05) - 2.3025851 * jax.random.uniform(streams_of[3], (POINTS,), jnp.float32) ** level_of(streams_of[3], (POINTS,), ((0, 32),), -0.2, 0.2)), 0.005, 0.05)
    batch_blocks = different_ones(streams_of[4], BATCHES, UB, BB, 0)
    tile_owner_keys = jax.random.split(jax.random.fold_in(streams_of[5], 1), REQS // R)
    tile_owner_turns = jax.random.permutation(jax.random.fold_in(streams_of[5], 3), REQS // R)
    tile_owner = jax.vmap(lambda own, number: deal_out(jax.random.fold_in(streams_of[5], 2), own, number, R, OWNERS, 1, CAP, 1))(tile_owner_keys, tile_owner_turns).reshape((REQS, 1))
    tile_slot = with_ends(jax.random.randint(streams_of[6], (REQS,), 0, TILE_DEV), jax.random.fold_in(streams_of[6], 1), 0, TILE_DEV - 1).astype(jnp.int32)
    batch_atoms = different_ones(streams_of[7], BATCHES, ATOM_GRP, NEAR, 0)
    batch_weights = with_ends(jax.random.randint(streams_of[8], (BATCHES, NEAR), 1, 9), jax.random.fold_in(streams_of[8], 1), 1, 8).astype(jnp.int32)
    atom_grid_index = with_ends(jax.random.randint(streams_of[9], (3, ATOMS), 0, GRIDN), jax.random.fold_in(streams_of[9], 1), 0, GRIDN - 1).astype(jnp.int32)
    return dict(orbitals=orbitals, dens_tiles=dens_tiles, point_coords=point_coords, point_weights=point_weights, batch_blocks=batch_blocks, tile_owner=tile_owner, tile_slot=tile_slot, batch_atoms=batch_atoms, batch_weights=batch_weights, atom_grid_index=atom_grid_index)


TOP_PRECISION = lax.Precision.HIGHEST


def wave_table(count):
    mode_ids = jnp.arange(count // 2, dtype=jnp.int32)
    return jnp.stack([mode_ids % 8, (mode_ids // 8) % 8, mode_ids // 64]).astype(jnp.float32)


def kernel_gains(count):
    wave_vecs = wave_table(count)
    squared = jnp.sum(wave_vecs * wave_vecs, axis=0)
    near_gain = 0.1 / (1.0 + 0.1 * squared)
    far_gain = 0.03 / (1.0 + 0.1 * squared)
    return jnp.concatenate([near_gain, near_gain]), jnp.concatenate([far_gain, far_gain])


def local_basis(coords, centre_points, wave_vecs, grid_extent):
    displace = coords[:, :, None, :] - centre_points[:, :, :, None]
    phases = jnp.einsum("cbnp,cm->bnpm", displace, wave_vecs, precision=TOP_PRECISION) * (2.0 * math.pi / grid_extent)
    envelope = jnp.exp(-2.0 * jnp.sum(displace * displace, axis=0) / (grid_extent * grid_extent))
    return envelope[..., None] * jnp.concatenate([jnp.cos(phases), jnp.sin(phases)], axis=-1)


def wave_values(coords, wave_vecs, grid_extent):
    phases = jnp.einsum("cbp,cm->bpm", coords, wave_vecs, precision=TOP_PRECISION) * (2.0 * math.pi / grid_extent)
    return jnp.concatenate([jnp.cos(phases), jnp.sin(phases)], axis=-1)


def reference(orbitals, dens_tiles, point_coords, point_weights, batch_blocks, tile_owner, tile_slot, batch_atoms, batch_weights, atom_grid_index):
    devices = N_GRP * N_DEV
    wave_vecs = wave_table(KM)
    near_gain, far_gain = kernel_gains(KM)
    atom_location = atom_grid_index.astype(jnp.float32)
    group_of = jnp.arange(devices, dtype=jnp.int32) // N_DEV
    tile_index = (group_of[:, None] * (TILE_DEV * N_DEV) + tile_owner[:, 0].reshape(devices, R) * TILE_DEV
                  + tile_slot.reshape(devices, R)).astype(jnp.int32)
    orbital_dev = orbitals.reshape(devices, BAT_DEV, PTS, BORB)
    coord_dev = point_coords.reshape(3, devices, BAT_DEV, PTS)
    weight_dev = point_weights.reshape(devices, BAT_DEV, PTS)
    block_dev = batch_blocks.reshape(devices, BAT_DEV, BB)
    atom_dev = (batch_atoms.reshape(devices, BAT_DEV, NEAR) + group_of[:, None, None] * ATOM_GRP).astype(jnp.int32)
    raw_weight = batch_weights.reshape(devices, BAT_DEV, NEAR).astype(jnp.float32)
    partition = raw_weight / jnp.sum(raw_weight, axis=2, keepdims=True)
    device_ids = jnp.arange(devices, dtype=jnp.int32)
    batch_ids = jnp.arange(BAT_DEV, dtype=jnp.int32)

    def basis_of(device):
        return local_basis(coord_dev[:, device], atom_location[:, atom_dev[device]], wave_vecs, GRIDN)

    def density_pass(moments, device):
        local_tiles = dens_tiles[tile_index[device]]

        def one_batch(batch_no):
            orbital = orbital_dev[device, batch_no]
            chosen = block_dev[device, batch_no]
            block_index = chosen[:, None] * UB + chosen[None, :]
            dens_block = local_tiles[block_index].transpose(0, 2, 1, 3).reshape(BORB, BORB)
            product = jnp.dot(orbital, dens_block, preferred_element_type=jnp.float32)
            return jnp.sum(product * orbital.astype(jnp.float32), axis=1)

        density = lax.map(one_batch, batch_ids)
        ebasis = basis_of(device)
        coeffs = partition[device][:, :, None] * jnp.einsum("bp,bnpk->bnk", weight_dev[device] * density, ebasis, precision=TOP_PRECISION)
        moments = moments.at[atom_dev[device].reshape(-1)].add(coeffs.reshape(BAT_DEV * NEAR, KM))
        return moments, density

    moments, density_all = lax.scan(density_pass, jnp.zeros((ATOMS, KM), jnp.float32), device_ids)
    atom_trig = wave_values(atom_location[:, None, :], wave_vecs, GRIDN)[0]
    structure = jnp.dot(moments[:, 0], atom_trig, precision=TOP_PRECISION)
    coef_near = near_gain[None, :] * moments
    far_coef = far_gain * structure

    def hamilton_pass(ham_sum, device):
        ebasis = basis_of(device)
        chosen_coef = coef_near[atom_dev[device]]
        near_val = jnp.sum(partition[device][:, :, None] * jnp.einsum("bnpk,bnk->bnp", ebasis, chosen_coef, precision=TOP_PRECISION), axis=1)
        far_val = jnp.einsum("bpk,k->bp", wave_values(coord_dev[:, device], wave_vecs, GRIDN), far_coef, precision=TOP_PRECISION)
        potential = near_val + far_val
        scaled_pot = weight_dev[device] * potential

        def one_batch(ham_local, batch_no):
            orbital = orbital_dev[device, batch_no]
            chosen = block_dev[device, batch_no]
            scaled_orb = (scaled_pot[batch_no][:, None] * orbital.astype(jnp.float32)).astype(jnp.bfloat16)
            ham_batch = lax.dot_general(orbital, scaled_orb, (((0,), (0,)), ((), ())), preferred_element_type=jnp.float32)
            pieces = ham_batch.reshape(BB, TB, BB, TB).transpose(0, 2, 1, 3).reshape(BB * BB, TB, TB)
            block_index = (chosen[:, None] * UB + chosen[None, :]).reshape(-1)
            return ham_local.at[block_index].add(pieces), None

        ham_local, unused = lax.scan(one_batch, jnp.zeros((R, TB, TB), jnp.float32), batch_ids)
        rounded = lax.optimization_barrier(ham_local.astype(jnp.bfloat16)).astype(jnp.float32)
        return ham_sum.at[tile_index[device]].add(rounded), potential

    ham_sum, potential_all = lax.scan(hamilton_pass, jnp.zeros((TILES, TB, TB), jnp.float32), device_ids)
    return density_all.reshape(-1), potential_all.reshape(-1), ham_sum.astype(jnp.bfloat16)
```

```python
import functools
import math

import jax
import jax.numpy as jnp
from jax import lax
from jax.experimental import pallas as pl
from jax.experimental.pallas import tpu as pltpu
from jax.sharding import PartitionSpec as P

TB = 128
KM = 512
GRIDN = 64
FXY = 64
FZ = KM // 2 // FXY
WAVES = 2 * FZ
MESH = pl.DeviceIdType.MESH
VM = pl.BlockSpec(memory_space=pltpu.VMEM)
SM = pl.BlockSpec(memory_space=pltpu.SMEM)
ANY = pl.BlockSpec(memory_space=pl.ANY)
f32, i32, bf16 = jnp.float32, jnp.int32, jnp.bfloat16


def turn_trig(turns):
    angle = (turns - jnp.round(turns)) * (2.0 * math.pi)
    return jnp.cos(angle), jnp.sin(angle)


def stack_split(value):
    high = value.astype(bf16)
    rest = (value - high.astype(f32)).astype(bf16)
    return jnp.concatenate([high, rest], axis=0)


def table_dot(both, high, low, turned):
    rows = both.shape[0] // 2
    dims = (((1,), (1 if turned else 0,)), ((), ()))
    out = lax.dot_general(both, high, dims, preferred_element_type=f32)
    fine = lax.dot_general(both[:rows], low, dims, preferred_element_type=f32)
    return out[:rows] + out[rows:] + fine


def lane_modes(shape):
    lane = lax.broadcasted_iota(i32, shape, 1)
    fx = (lane & 7).astype(f32)
    fy = ((lane >> 3) & 7).astype(f32)
    return lane, fx, fy


def half_turn(value, first, second):
    lane = lax.broadcasted_iota(i32, value.shape, 1)
    return pltpu.roll(value, FXY, 1) * jnp.where(lane < FXY, first, second)


def region_kernel(
    n, regions, parts, listed, near, orb, meta, coords, weights, dens, grid_s,
    density, potential, scaled, meta_all, land, flip,
    meta_v, meta_s, coords_all, weights_all, tiles, block,
    t1h, t1l, t2, spread, wrow, far, lhs_far, waves, part, part_in,
    macc, moments, moments_in, near_acc, qacc, charge, charge_in,
    pack_sem, local_sem, send, recv, fsend, frecv, wsend, wrecv,
    dsend, drecv, tsend, trecv, qsend, qrecv, ready,
):
    me = lax.axis_index("dev")
    grp = lax.axis_index("grp")
    bits = n.bit_length() - 1
    batches, points, width = orb.shape
    here = batches * points
    held = width // TB
    union = math.isqrt(listed)
    stored = dens.shape[0]
    atoms = grid_s.shape[1]
    rows = spread.shape[0]
    piece = points // parts
    lanes = charge.shape[2]
    block_at = listed
    atom_at = block_at + batches * held
    weight_at = atom_at + batches * near

    packs = []
    for b in range(batches):
        for u in range(held):
            copy = pltpu.make_async_copy(
                orb.at[b, :, pl.ds(u * TB, TB)], land.at[0, b, u], pack_sem.at[b, u]
            )
            copy.start()
            packs.append(copy)
    own = [pltpu.make_async_copy(dens, tiles.at[pl.ds(0, stored)], local_sem.at[0])]
    own[0].start()
    barrier = pltpu.get_barrier_semaphore()
    for mask in range(1, n):
        pl.semaphore_signal(barrier, inc=1, device_id={"dev": me ^ mask}, device_id_type=MESH)
    for step in range(1, regions):
        pl.semaphore_signal(
            barrier, inc=1, device_id={"grp": lax.rem(grp + step, regions)}, device_id_type=MESH
        )
    tiles[stored] = jnp.zeros((TB, TB), bf16)
    macc[...] = jnp.zeros_like(macc)
    qacc[...] = jnp.zeros_like(qacc)
    for copy in packs:
        copy.wait()
    pl.semaphore_wait(barrier, n + regions - 2)

    def remote(src, dst, ssem, rsem, **where):
        return pltpu.make_async_remote_copy(
            src_ref=src, dst_ref=dst, send_sem=ssem, recv_sem=rsem,
            device_id=where, device_id_type=MESH,
        )

    def order_of(b):
        return list(range(bits)) if b % 2 == 0 else list(range(bits))[::-1]

    def landing(mask, b, c):
        return land.at[mask, b, :, pl.ds(c * piece, piece), :]

    def orb_copy(b, stage, mask, c):
        bit = 1 << order_of(b)[stage]
        got = mask ^ bit
        return remote(
            landing(mask, b, c), landing(got, b, c), send.at[b, c, got], recv.at[b, c, got],
            dev=me ^ bit,
        )

    started = []
    feats = []
    pairs = ((meta, meta_v), (coords, coords_all), (weights, weights_all))
    for mask in range(1, n):
        for k, (src, dst) in enumerate(pairs):
            copy = remote(src, dst.at[me], fsend.at[k, mask], frecv.at[k, mask], dev=me ^ mask)
            copy.start()
            feats.append(copy)
    for stage in range(bits):
        for b in range(batches):
            for c in range(parts):
                copy = orb_copy(b, stage, 0, c)
                copy.start()
                started.append(copy)
    for k, (src, dst) in enumerate(pairs, 1):
        copy = pltpu.make_async_copy(src, dst.at[me], local_sem.at[k])
        copy.start()
        own.append(copy)
    for mask in range(1, n):
        pl.semaphore_signal(ready, inc=1, device_id={"dev": me ^ mask}, device_id_type=MESH)

    shape = (rows, TB)
    lane, fx, fy = lane_modes(shape)
    row = lax.broadcasted_iota(i32, shape, 0)
    place = []
    for c in range(3):
        at = jnp.zeros(shape, f32)
        for a in range(atoms):
            at = jnp.where(row == a, grid_s[c, a].astype(f32), at)
        place.append(at)
    for z in range(FZ):
        turns = (fx * place[0] + fy * place[1] + place[2] * float(z)) * (1.0 / GRIDN)
        cos, sin = turn_trig(turns)
        gain = 0.03 / (1.0 + 0.1 * (fx * fx + fy * fy + float(z * z)))
        wave = jnp.where(lane < FXY, cos, sin) * gain
        waves[grp, z] = jnp.where(row < atoms, wave, 0.0)
    wave_copies = []
    for step in range(1, regions):
        copy = remote(
            waves.at[grp], waves.at[grp], wsend.at[step], wrecv.at[step],
            grp=lax.rem(grp + step, regions),
        )
        copy.start()
        wave_copies.append(copy)

    for copy in feats + own:
        copy.wait()
    codes = meta_v[...]
    at = lax.broadcasted_iota(i32, codes.shape, 2)
    local = codes - me * stored
    mine = (local >= 0) & (local < stored)
    meta_v[...] = jnp.where(at < listed, jnp.where(mine, local, stored), codes)
    moved = [
        pltpu.make_async_copy(meta_v, meta_s, local_sem.at[0]),
        pltpu.make_async_copy(meta_v, meta_all, local_sem.at[1]),
    ]
    for copy in moved:
        copy.start()

    def mask_cols(mask, first, count):
        return pl.ds(pl.multiple_of(mask * here + first, TB), count)

    def tables(mask, carry):
        e = me ^ mask
        cols = mask_cols(mask, 0, here)
        step = lax.broadcasted_iota(i32, (8, here), 0)
        where = coords_all[e]
        first = []
        for c in range(2):
            turns = step.astype(f32) * where[c : c + 1, :] * (1.0 / GRIDN)
            first.append(turn_trig(turns))
        (cx, sx), (cy, sy) = first
        for y in range(0, 8, 2):
            cos, sin = [], []
            for q in (y, y + 1):
                cq, sq = cy[q : q + 1, :], sy[q : q + 1, :]
                cos.append(cx * cq - sx * sq)
                sin.append(sx * cq + cx * sq)
            for base, wave in ((0, cos), (FXY, sin)):
                wave = jnp.concatenate(wave, axis=0)
                high = wave.astype(bf16)
                t1h[base + y * 8 : base + y * 8 + 16, cols] = high
                t1l[base + y * 8 : base + y * 8 + 16, cols] = (wave - high.astype(f32)).astype(bf16)
        step = lax.broadcasted_iota(i32, (WAVES, here), 0)
        times = jnp.where(step < FZ, step, step - FZ).astype(f32)
        cz, sz = turn_trig(times * where[2:3, :] * (1.0 / GRIDN))
        t2[:, cols] = jnp.where(step < FZ, cz, sz)
        wrow[:, cols] = weights_all[e]
        row = lax.broadcasted_iota(i32, (rows, points), 0)
        for b in range(batches):
            total = jnp.int32(0)
            for k in range(near):
                total = total + meta_s[e, 0, weight_at + b * near + k]
            share = jnp.zeros((rows, points), i32)
            spot = [jnp.zeros((rows, points), f32) for c in range(3)]
            for a in range(atoms):
                part_of = jnp.int32(0)
                for k in range(near):
                    weight = meta_s[e, 0, weight_at + b * near + k]
                    part_of = part_of + jnp.where(
                        meta_s[e, 0, atom_at + b * near + k] == a, weight, 0
                    )
                share = jnp.where(row == a, part_of, share)
                for c in range(3):
                    spot[c] = jnp.where(row == a, grid_s[c, a].astype(f32), spot[c])
            squared = jnp.zeros((rows, points), f32)
            for c in range(3):
                gone = where[c : c + 1, b * points : (b + 1) * points] - spot[c]
                squared = squared + gone * gone
            fraction = share.astype(f32) / jnp.full((rows, points), total.astype(f32))
            spread[:, mask_cols(mask, b * points, points)] = fraction * jnp.exp(
                squared * (-2.0 / (GRIDN * GRIDN))
            )
        return carry

    def far_rows():
        for z in range(FZ):
            for g in range(regions):
                cs = waves[g, z]
                for j, value in ((z, cs), (FZ + z, half_turn(cs, 1.0, -1.0))):
                    high = value.astype(bf16)
                    first = (j * regions + g) * rows
                    lhs_far[0, first : first + rows, :] = value
        return None

    def far_cols(q, carry):
        cols = pl.ds(pl.multiple_of(q * 2 * TB, 2 * TB), 2 * TB)
        high, low = t1h[:, cols], t1l[:, cols]
        every = regions * rows
        total = jnp.zeros((every, 2 * TB), f32)
        for j in range(WAVES):
            value = lhs_far[0, j * every : (j + 1) * every, :]
            out = table_dot(stack_split(value), high, low, False)
            total = total + out * t2[j : j + 1, cols]
        far[:, cols] = total
        return carry

    def assemble(mask, b):
        e = me ^ mask

        def block_row(i, carry):
            first = meta_s[e, 0, block_at + b * held + i] * union
            for j in range(held):
                index = meta_s[e, 0, first + meta_s[e, 0, block_at + b * held + j]]
                block[b, pl.ds(pl.multiple_of(i * TB, TB), TB), j * TB : (j + 1) * TB] = tiles[index]
            return carry

        lax.fori_loop(0, held, block_row, 0)

    def process(mask, b, c):
        at = slice(c * piece, (c + 1) * piece)
        cols = slice(mask * here + b * points + c * piece, mask * here + b * points + (c + 1) * piece)
        orbital = [land[mask, b, u, at, :] for u in range(held)]
        lhs = jnp.concatenate(orbital, axis=1)
        total = jnp.zeros((piece, TB), f32)
        for v in range(0, held, 2):
            some = min(2, held - v)
            product = jnp.dot(lhs, block[b, :, v * TB : (v + some) * TB], preferred_element_type=f32)
            for t in range(some):
                total = total + product[:, t * TB : (t + 1) * TB] * orbital[v + t].astype(f32)
        line = jnp.sum(total.T, axis=0, keepdims=True)
        part[mask, :, b * points + c * piece : b * points + (c + 1) * piece] = line
        source = spread[:, cols] * (wrow[:, cols] * line)
        folded = source[:, 0:TB]
        for q in range(TB, piece, TB):
            folded = folded + source[:, q : q + TB]
        qacc[...] = qacc[...] + folded
        waved = jnp.concatenate([source * t2[j : j + 1, cols] for j in range(WAVES)], axis=0)
        macc[...] = macc[...] + table_dot(stack_split(waved), t1h[:, cols], t1l[:, cols], True)

    def turn(mask, b, c):
        at = slice(c * piece, (c + 1) * piece)
        for u in range(held):
            flip[mask, b, u * TB : (u + 1) * TB, at] = land[mask, b, u, at, :].T

    density_sends = []

    def send_density(mask):
        if mask:
            copy = remote(
                part.at[mask], part_in.at[mask], dsend.at[mask], drecv.at[mask], dev=me ^ mask
            )
            copy.start()
            density_sends.append(copy)

    rounds = [(None, [0] * batches)]
    for stage in range(bits):
        for low in range(1 << stage):
            masks = []
            for b in range(batches):
                got = 1 << order_of(b)[stage]
                for t in range(stage):
                    if low >> t & 1:
                        got ^= 1 << order_of(b)[t]
                masks.append(got)
            rounds.append((stage, masks))
    done = {}
    for copy in moved:
        copy.wait()
    lax.fori_loop(0, n, tables, 0)
    for number, (stage, masks) in enumerate(rounds):
        last = number == len(rounds) - 1
        for b in range(batches):
            assemble(masks[b], b)
        if last:
            for copy in wave_copies:
                copy.wait()
            far_rows()
            lax.fori_loop(0, n * here // (2 * TB), far_cols, 0)
        for c in range(parts):
            for b in range(batches):
                mask = masks[b]
                if stage is not None:
                    there = landing(mask, b, c)
                    bit = 1 << order_of(b)[stage]
                    remote(
                        there, there, send.at[b, c, mask], recv.at[b, c, mask], dev=me ^ bit
                    ).wait_recv()
                    for later in range(stage + 1, bits):
                        copy = orb_copy(b, later, mask, c)
                        copy.start()
                        started.append(copy)
                process(mask, b, c)
                if not last:
                    turn(mask, b, c)
        for mask in masks:
            done[mask] = done.get(mask, 0) + 1
            if done[mask] == batches and not last:
                send_density(mask)

    column = jnp.sum(qacc[...], axis=1, keepdims=True)
    shape = (rows, lanes)
    lane = lax.broadcasted_iota(i32, shape, 1)
    row = lax.broadcasted_iota(i32, shape, 0)
    spot = jnp.where(lane == grp * rows + row, jnp.broadcast_to(column, shape), 0.0)
    mine = jnp.sum(spot, axis=0, keepdims=True)
    charge[0] = mine
    pl.semaphore_wait(ready, n - 1)
    charge_copies = []
    for step in reversed(range(regions)):
        for mask in reversed(range(n)):
            if step or mask:
                slot = step * n + mask
                copy = remote(
                    charge.at[0], charge_in.at[slot], qsend.at[slot], qrecv.at[slot],
                    grp=lax.rem(grp + step, regions), dev=me ^ mask,
                )
                copy.start()
                charge_copies.append(copy)
    waved = macc[...]
    sums = []
    for z in range(FZ):
        cos = waved[z * rows : (z + 1) * rows]
        sin = waved[(FZ + z) * rows : (FZ + z + 1) * rows]
        sums.append(cos + half_turn(sin, -1.0, 1.0))
        moments[z] = sums[z]
    moment_copies = []
    for mask in range(1, n):
        copy = remote(
            moments, moments_in.at[mask], tsend.at[mask], trecv.at[mask], dev=me ^ mask
        )
        copy.start()
        moment_copies.append(copy)
    for mask in dict.fromkeys(rounds[-1][1]):
        send_density(mask)
    for copy in moment_copies:
        copy.wait()
    lane, fx, fy = lane_modes((rows, TB))
    first, second = [], []
    for z in range(FZ):
        for mask in range(1, n):
            sums[z] = sums[z] + moments_in[mask, z]
        gain = 0.1 / (1.0 + 0.1 * (fx * fx + fy * fy + float(z * z)))
        value = sums[z] * gain
        first.append(value)
        second.append(half_turn(value, 1.0, -1.0))
    both = stack_split(jnp.concatenate(first + second, axis=0))

    def near_cols(first, count):
        cols = pl.ds(first, count)
        out = table_dot(both, t1h[:, cols], t1l[:, cols], False)
        total = jnp.zeros((rows, count), f32)
        for j in range(WAVES):
            total = total + out[j * rows : (j + 1) * rows] * t2[j : j + 1, cols]
        near_acc[:, cols] = jnp.sum(total * spread[:, cols], axis=0, keepdims=True)

    for q in range(0, n * here, here):
        near_cols(q, here)
    for c in range(parts):
        for b in range(batches):
            turn(rounds[-1][1][b], b, c)
    for copy in density_sends:
        copy.wait()
    rho = part[0]
    for mask in range(1, n):
        rho = rho + part_in[mask]
    density[...] = rho
    for copy in started:
        copy.wait_send()

    for copy in charge_copies:
        copy.wait()
    total = mine
    for slot in range(1, n * regions):
        total = total + charge_in[slot]
    every = regions * rows
    shape = (every, lanes)
    lane = lax.broadcasted_iota(i32, shape, 1)
    row = lax.broadcasted_iota(i32, shape, 0)
    spot = jnp.where(lane == row, jnp.broadcast_to(total, shape), 0.0)
    column = jnp.sum(spot, axis=1, keepdims=True)
    for q in range(0, n * here, here):
        cols = slice(q, q + here)
        field = near_acc[:, cols] + jnp.sum(far[:, cols] * column, axis=0, keepdims=True)
        if q == 0:
            potential[...] = field
        scaled[q // here] = wrow[:, cols] * field


def hamilton_kernel(
    meta, land, flip, scaled, density8, potential8, out, density, potential, totals,
    *, listed,
):
    n, batches, held, points = land.shape[:4]
    union = math.isqrt(listed)
    stored = out.shape[0]
    block_at = listed
    me = lax.axis_index("dev")
    banks = totals.shape[0]
    for q in range(density.shape[0]):
        density[q : q + 1, :] = density8[0:1, q * TB : (q + 1) * TB]
        potential[q : q + 1, :] = potential8[0:1, q * TB : (q + 1) * TB]

    def clear(t, carry):
        for k in range(banks):
            totals[k, t] = jnp.zeros((TB, TB), f32)
        return carry

    lax.fori_loop(0, stored + 1, clear, 0)

    def one(item, carry):
        mask = item // batches
        b = item - mask * batches
        e = me ^ mask
        line = scaled[mask, :, pl.ds(pl.multiple_of(b * points, TB), points)]
        column = jnp.broadcast_to(line, (TB, points)).T
        right = [
            (column * land[mask, b, j].astype(f32)).astype(bf16) for j in range(held)
        ]
        left = flip[mask, b]
        spots = [meta[e, 0, block_at + b * held + i] for i in range(held)]
        turn = 0
        for j in range(0, held, 2):
            some = min(2, held - j)
            product = jnp.dot(
                left, jnp.concatenate(right[j : j + some], axis=1), preferred_element_type=f32
            )
            for i in range(held):
                for t in range(some):
                    slot = meta[e, 0, spots[i] * union + spots[j + t]]
                    tile = product[i * TB : (i + 1) * TB, t * TB : (t + 1) * TB]
                    totals[turn % banks, slot] = totals[turn % banks, slot] + tile
                    turn += 1
        return carry

    lax.fori_loop(0, n * batches, one, 0)

    def finish(t, carry):
        value = totals[0, t]
        for k in range(1, banks):
            value = value + totals[k, t]
        out[t] = value.astype(bf16)
        return carry

    lax.fori_loop(0, stored, finish, 0)


def on_device(
    n, regions, orbitals, dens_tiles, point_coords, point_weights, batch_blocks,
    tile_owner, tile_slot, batch_atoms, batch_weights, atom_grid_index,
):
    stored = dens_tiles.shape[0]
    listed = tile_slot.shape[0]
    batches, points, width = orbitals.shape
    near = batch_atoms.shape[1]
    here = batches * points
    held = width // TB
    atoms = atom_grid_index.shape[1]
    rows = -(-atoms // 8) * 8
    parts = 2
    banks = 2
    code = tile_owner[:, 0] * stored + tile_slot
    facts = [code, batch_blocks.reshape(-1), batch_atoms.reshape(-1), batch_weights.reshape(-1)]
    count = sum(fact.shape[0] for fact in facts)
    wide = -(-count // TB) * TB
    meta = jnp.pad(jnp.concatenate(facts), (0, wide - count))[None]
    lanes = -(-regions * rows // TB) * TB
    kept = 4 * n * batches * points * width + 64 * n * here + (1 << 20)
    grant = (62 << 20) - kept
    S = jax.ShapeDtypeStruct
    dma = pltpu.SemaphoreType.DMA
    V = pltpu.VMEM
    density, potential, scaled, meta_all, land, flip = pl.pallas_call(
        functools.partial(region_kernel, n, regions, parts, listed, near),
        out_shape=(
            V((1, here), f32),
            V((1, here), f32),
            V((n, 1, here), f32),
            S((n, 1, wide), i32),
            V((n, batches, held, points, TB), bf16),
            V((n, batches, width, points), bf16),
        ),
        in_specs=[ANY, VM, VM, VM, ANY, SM],
        out_specs=(VM, VM, VM, ANY, VM, VM),
        scratch_shapes=[
            V((n, 1, wide), i32),
            pltpu.SMEM((n, 1, wide), i32),
            V((n, 3, here), f32),
            V((n, 1, here), f32),
            V((stored + 1, TB, TB), bf16),
            V((batches, width, width), bf16),
            V((2 * FXY, n * here), bf16),
            V((2 * FXY, n * here), bf16),
            V((WAVES, n * here), f32),
            V((rows, n * here), f32),
            V((1, n * here), f32),
            V((regions * rows, n * here), f32),
            V((1, WAVES * regions * rows, TB), f32),
            V((regions, FZ, rows, TB), f32),
            V((n, 1, here), f32),
            V((n, 1, here), f32),
            V((WAVES * rows, TB), f32),
            V((FZ, rows, TB), f32),
            V((n, FZ, rows, TB), f32),
            V((1, n * here), f32),
            V((rows, TB), f32),
            V((1, 1, lanes), f32),
            V((n * regions, 1, lanes), f32),
            dma((batches, held)),
            dma((4,)),
            dma((batches, parts, n)), dma((batches, parts, n)),
            dma((3, n)), dma((3, n)),
            dma((regions,)), dma((regions,)),
            dma((n,)), dma((n,)), dma((n,)), dma((n,)),
            dma((n * regions,)), dma((n * regions,)),
            pltpu.SemaphoreType.REGULAR,
        ],
        compiler_params=pltpu.CompilerParams(
            collective_id=0, has_side_effects=True, vmem_limit_bytes=grant
        ),
        name="region",
    )(
        orbitals, meta, point_coords, point_weights.reshape(1, here), dens_tiles, atom_grid_index,
    )
    density, potential, scaled, land, flip = [
        pltpu.with_memory_space_constraint(value, pltpu.VMEM)
        for value in (density, potential, scaled, land, flip)
    ]
    ham_tiles, density, potential = pl.pallas_call(
        functools.partial(hamilton_kernel, listed=listed),
        out_shape=(
            S((stored, TB, TB), bf16), S((here // TB, TB), f32), S((here // TB, TB), f32),
        ),
        in_specs=[SM, VM, VM, VM, VM, VM],
        out_specs=(VM, VM, VM),
        scratch_shapes=[V((banks, stored + 1, TB, TB), f32)],
        compiler_params=pltpu.CompilerParams(vmem_limit_bytes=grant),
        name="hamilton",
    )(meta_all, land, flip, scaled, density, potential)
    return density.reshape(-1), potential.reshape(-1), ham_tiles


def solution(mesh):
    body = functools.partial(on_device, mesh.shape["dev"], mesh.shape["grp"])
    in_specs = (
        P(("grp", "dev"), None, None),
        P(("grp", "dev"), None, None),
        P(None, ("grp", "dev")),
        P(("grp", "dev")),
        P(("grp", "dev"), None),
        P(("grp", "dev"), None),
        P(("grp", "dev")),
        P(("grp", "dev"), None),
        P(("grp", "dev"), None),
        P(None, "grp"),
    )
    out_specs = (P(("grp", "dev")), P(("grp", "dev")), P(("grp", "dev"), None, None))
    return jax.shard_map(body, mesh=mesh, in_specs=in_specs, out_specs=out_specs, check_vma=False)
```

```python
import functools
import math

import jax
import jax.numpy as jnp
from jax import lax
from jax.experimental import pallas as pl
from jax.experimental.pallas import tpu as pltpu
from jax.sharding import PartitionSpec as P

TB = 128
KM = 512
GRIDN = 64
FXY = 64
FZ = KM // 2 // FXY
WAVES = 2 * FZ
MESH = pl.DeviceIdType.MESH
VM = pl.BlockSpec(memory_space=pltpu.VMEM)
SM = pl.BlockSpec(memory_space=pltpu.SMEM)
ANY = pl.BlockSpec(memory_space=pl.ANY)
f32, i32, bf16 = jnp.float32, jnp.int32, jnp.bfloat16


def turn_trig(turns):
    angle = (turns - jnp.round(turns)) * (2.0 * math.pi)
    return jnp.cos(angle), jnp.sin(angle)


def stack_split(value):
    high = value.astype(bf16)
    rest = (value - high.astype(f32)).astype(bf16)
    return jnp.concatenate([high, rest], axis=0)


def table_dot(both, high, low, turned):
    rows = both.shape[0] // 2
    dims = (((1,), (1 if turned else 0,)), ((), ()))
    out = lax.dot_general(both, high, dims, preferred_element_type=f32)
    fine = lax.dot_general(both[:rows], low, dims, preferred_element_type=f32)
    return out[:rows] + out[rows:] + fine


def lane_modes(shape):
    lane = lax.broadcasted_iota(i32, shape, 1)
    fx = (lane & 7).astype(f32)
    fy = ((lane >> 3) & 7).astype(f32)
    return lane, fx, fy


def half_turn(value, first, second):
    lane = lax.broadcasted_iota(i32, value.shape, 1)
    return pltpu.roll(value, FXY, 1) * jnp.where(lane < FXY, first, second)


def region_kernel(
    n, regions, parts, orb, owner, slot, blocks, batch_atoms, batch_weights, coords, weights,
    dens, grid_s,
    density, potential, scaled, meta_all, land, flip,
    facts, meta_v, meta_s, coords_all, weights_all, tiles, block,
    t1h, t1l, t2, spread, wrow, far, lhs_far, waves, part, part_in,
    macc, moments, moments_in, near_acc, qacc, charge, charge_in,
    pack_sem, local_sem, send, recv, fsend, frecv, wsend, wrecv,
    dsend, drecv, tsend, trecv, qsend, qrecv, ready,
):
    me = lax.axis_index("dev")
    grp = lax.axis_index("grp")
    bits = n.bit_length() - 1
    batches, points, width = orb.shape
    here = batches * points
    held = width // TB
    stored = dens.shape[0]
    atoms = grid_s.shape[1]
    rows = spread.shape[0]
    piece = points // parts
    lanes = charge.shape[2]
    listed = owner.shape[1]
    near = batch_atoms.shape[1]
    union = math.isqrt(listed)
    block_at, atom_at, weight_at = 1, 1 + batches, 1 + 2 * batches

    packs = []
    for b in range(batches):
        for u in range(held):
            copy = pltpu.make_async_copy(
                orb.at[b, :, pl.ds(u * TB, TB)], land.at[0, b, u], pack_sem.at[b, u]
            )
            copy.start()
            packs.append(copy)
    own = [pltpu.make_async_copy(dens, tiles.at[pl.ds(0, stored)], local_sem.at[0])]
    own[0].start()
    barrier = pltpu.get_barrier_semaphore()
    for mask in range(1, n):
        pl.semaphore_signal(barrier, inc=1, device_id={"dev": me ^ mask}, device_id_type=MESH)
    for step in range(1, regions):
        pl.semaphore_signal(
            barrier, inc=1, device_id={"grp": lax.rem(grp + step, regions)}, device_id_type=MESH
        )
    facts[...] = jnp.zeros_like(facts)
    facts[0:1, 0:listed] = owner[...] * stored + slot[...]
    facts[block_at : block_at + batches, 0:held] = blocks[...]
    facts[atom_at : atom_at + batches, 0:near] = batch_atoms[...]
    facts[weight_at : weight_at + batches, 0:near] = batch_weights[...]
    tiles[stored] = jnp.zeros((TB, TB), bf16)
    macc[...] = jnp.zeros_like(macc)
    qacc[...] = jnp.zeros_like(qacc)
    for copy in packs:
        copy.wait()
    pl.semaphore_wait(barrier, n + regions - 2)

    def remote(src, dst, ssem, rsem, **where):
        return pltpu.make_async_remote_copy(
            src_ref=src, dst_ref=dst, send_sem=ssem, recv_sem=rsem,
            device_id=where, device_id_type=MESH,
        )

    def order_of(b):
        return list(range(bits)) if b % 2 == 0 else list(range(bits))[::-1]

    def landing(mask, b, c):
        return land.at[mask, b, :, pl.ds(c * piece, piece), :]

    def orb_copy(b, stage, mask, c):
        bit = 1 << order_of(b)[stage]
        got = mask ^ bit
        return remote(
            landing(mask, b, c), landing(got, b, c), send.at[b, c, got], recv.at[b, c, got],
            dev=me ^ bit,
        )

    started = []
    feats = []
    pairs = ((facts, meta_v), (coords, coords_all), (weights, weights_all))
    for mask in range(1, n):
        for k, (src, dst) in enumerate(pairs):
            copy = remote(src, dst.at[me], fsend.at[k, mask], frecv.at[k, mask], dev=me ^ mask)
            copy.start()
            feats.append(copy)
    for stage in range(bits):
        for b in range(batches):
            for c in range(parts):
                copy = orb_copy(b, stage, 0, c)
                copy.start()
                started.append(copy)
    for k, (src, dst) in enumerate(pairs, 1):
        copy = pltpu.make_async_copy(src, dst.at[me], local_sem.at[k])
        copy.start()
        own.append(copy)
    for mask in range(1, n):
        pl.semaphore_signal(ready, inc=1, device_id={"dev": me ^ mask}, device_id_type=MESH)

    shape = (rows, TB)
    lane, fx, fy = lane_modes(shape)
    row = lax.broadcasted_iota(i32, shape, 0)
    place = []
    for c in range(3):
        at = jnp.zeros(shape, f32)
        for a in range(atoms):
            at = jnp.where(row == a, grid_s[c, a].astype(f32), at)
        place.append(at)
    for z in range(FZ):
        turns = (fx * place[0] + fy * place[1] + place[2] * float(z)) * (1.0 / GRIDN)
        cos, sin = turn_trig(turns)
        gain = 0.03 / (1.0 + 0.1 * (fx * fx + fy * fy + float(z * z)))
        wave = jnp.where(lane < FXY, cos, sin) * gain
        waves[grp, z] = jnp.where(row < atoms, wave, 0.0)
    wave_copies = []
    for step in range(1, regions):
        copy = remote(
            waves.at[grp], waves.at[grp], wsend.at[step], wrecv.at[step],
            grp=lax.rem(grp + step, regions),
        )
        copy.start()
        wave_copies.append(copy)

    for copy in feats + own:
        copy.wait()
    codes = meta_v[...]
    at = lax.broadcasted_iota(i32, codes.shape, 1)
    local = codes - me * stored
    mine = (local >= 0) & (local < stored)
    meta_all[...] = jnp.where(at == 0, jnp.where(mine, local, stored), codes)
    moved = [pltpu.make_async_copy(meta_all, meta_s, local_sem.at[0])]
    for copy in moved:
        copy.start()

    def mask_cols(mask, first, count):
        return pl.ds(pl.multiple_of(mask * here + first, TB), count)

    def tables(mask, carry):
        e = me ^ mask
        cols = mask_cols(mask, 0, here)
        step = lax.broadcasted_iota(i32, (8, here), 0)
        where = coords_all[e]
        first = []
        for c in range(2):
            turns = step.astype(f32) * where[c : c + 1, :] * (1.0 / GRIDN)
            first.append(turn_trig(turns))
        (cx, sx), (cy, sy) = first
        for y in range(0, 8, 2):
            cos, sin = [], []
            for q in (y, y + 1):
                cq, sq = cy[q : q + 1, :], sy[q : q + 1, :]
                cos.append(cx * cq - sx * sq)
                sin.append(sx * cq + cx * sq)
            for base, wave in ((0, cos), (FXY, sin)):
                wave = jnp.concatenate(wave, axis=0)
                high = wave.astype(bf16)
                t1h[base + y * 8 : base + y * 8 + 16, cols] = high
                t1l[base + y * 8 : base + y * 8 + 16, cols] = (wave - high.astype(f32)).astype(bf16)
        step = lax.broadcasted_iota(i32, (WAVES, here), 0)
        times = jnp.where(step < FZ, step, step - FZ).astype(f32)
        cz, sz = turn_trig(times * where[2:3, :] * (1.0 / GRIDN))
        t2[:, cols] = jnp.where(step < FZ, cz, sz)
        wrow[:, cols] = weights_all[e]
        row = lax.broadcasted_iota(i32, (rows, points), 0)
        for b in range(batches):
            total = jnp.int32(0)
            for k in range(near):
                total = total + meta_s[e, weight_at + b, k]
            share = jnp.zeros((rows, points), i32)
            spot = [jnp.zeros((rows, points), f32) for c in range(3)]
            for a in range(atoms):
                part_of = jnp.int32(0)
                for k in range(near):
                    weight = meta_s[e, weight_at + b, k]
                    part_of = part_of + jnp.where(
                        meta_s[e, atom_at + b, k] == a, weight, 0
                    )
                share = jnp.where(row == a, part_of, share)
                for c in range(3):
                    spot[c] = jnp.where(row == a, grid_s[c, a].astype(f32), spot[c])
            squared = jnp.zeros((rows, points), f32)
            for c in range(3):
                gone = where[c : c + 1, b * points : (b + 1) * points] - spot[c]
                squared = squared + gone * gone
            fraction = share.astype(f32) / jnp.full((rows, points), total.astype(f32))
            spread[:, mask_cols(mask, b * points, points)] = fraction * jnp.exp(
                squared * (-2.0 / (GRIDN * GRIDN))
            )
        return carry

    def far_rows():
        for z in range(FZ):
            for g in range(regions):
                cs = waves[g, z]
                for j, value in ((z, cs), (FZ + z, half_turn(cs, 1.0, -1.0))):
                    first = (j * regions + g) * rows
                    lhs_far[0, first : first + rows, :] = value
        return None

    def far_cols(q, carry):
        cols = pl.ds(pl.multiple_of(q * 2 * TB, 2 * TB), 2 * TB)
        high, low = t1h[:, cols], t1l[:, cols]
        every = regions * rows
        total = jnp.zeros((every, 2 * TB), f32)
        for j in range(WAVES):
            value = lhs_far[0, j * every : (j + 1) * every, :]
            out = table_dot(stack_split(value), high, low, False)
            total = total + out * t2[j : j + 1, cols]
        far[:, cols] = total
        return carry

    def assemble(mask, b):
        e = me ^ mask

        def block_row(i, carry):
            first = meta_s[e, block_at + b, i] * union
            for j in range(held):
                index = meta_s[e, 0, first + meta_s[e, block_at + b, j]]
                block[b, pl.ds(pl.multiple_of(i * TB, TB), TB), j * TB : (j + 1) * TB] = tiles[index]
            return carry

        lax.fori_loop(0, held, block_row, 0)

    def process(mask, b, c):
        at = slice(c * piece, (c + 1) * piece)
        cols = slice(mask * here + b * points + c * piece, mask * here + b * points + (c + 1) * piece)
        orbital = [land[mask, b, u, at, :] for u in range(held)]
        lhs = jnp.concatenate(orbital, axis=1)
        total = jnp.zeros((piece, TB), f32)
        for v in range(0, held, 2):
            some = min(2, held - v)
            product = jnp.dot(lhs, block[b, :, v * TB : (v + some) * TB], preferred_element_type=f32)
            for t in range(some):
                total = total + product[:, t * TB : (t + 1) * TB] * orbital[v + t].astype(f32)
        line = jnp.sum(total.T, axis=0, keepdims=True)
        part[mask, :, b * points + c * piece : b * points + (c + 1) * piece] = line
        source = spread[:, cols] * (wrow[:, cols] * line)
        folded = source[:, 0:TB]
        for q in range(TB, piece, TB):
            folded = folded + source[:, q : q + TB]
        qacc[...] = qacc[...] + folded
        waved = jnp.concatenate([source * t2[j : j + 1, cols] for j in range(WAVES)], axis=0)
        macc[...] = macc[...] + table_dot(stack_split(waved), t1h[:, cols], t1l[:, cols], True)

    def turn(mask, b, c):
        at = slice(c * piece, (c + 1) * piece)
        for u in range(held):
            flip[mask, b, u * TB : (u + 1) * TB, at] = land[mask, b, u, at, :].T

    density_sends = []

    def send_density(mask):
        if mask:
            copy = remote(
                part.at[mask], part_in.at[mask], dsend.at[mask], drecv.at[mask], dev=me ^ mask
            )
            copy.start()
            density_sends.append(copy)

    rounds = [(None, [0] * batches)]
    for stage in range(bits):
        for low in range(1 << stage):
            masks = []
            for b in range(batches):
                got = 1 << order_of(b)[stage]
                for t in range(stage):
                    if low >> t & 1:
                        got ^= 1 << order_of(b)[t]
                masks.append(got)
            rounds.append((stage, masks))
    done = {}
    for copy in moved:
        copy.wait()
    lax.fori_loop(0, n, tables, 0)
    for number, (stage, masks) in enumerate(rounds):
        last = number == len(rounds) - 1
        for b in range(batches):
            assemble(masks[b], b)
        if last:
            for copy in wave_copies:
                copy.wait()
            far_rows()
            lax.fori_loop(0, n * here // (2 * TB), far_cols, 0)
        for c in range(parts):
            for b in range(batches):
                mask = masks[b]
                if stage is not None:
                    there = landing(mask, b, c)
                    bit = 1 << order_of(b)[stage]
                    remote(
                        there, there, send.at[b, c, mask], recv.at[b, c, mask], dev=me ^ bit
                    ).wait_recv()
                    for later in range(stage + 1, bits):
                        copy = orb_copy(b, later, mask, c)
                        copy.start()
                        started.append(copy)
                process(mask, b, c)
                if not last:
                    turn(mask, b, c)
        for mask in masks:
            done[mask] = done.get(mask, 0) + 1
            if done[mask] == batches and not last:
                send_density(mask)

    column = jnp.sum(qacc[...], axis=1, keepdims=True)
    shape = (rows, lanes)
    lane = lax.broadcasted_iota(i32, shape, 1)
    row = lax.broadcasted_iota(i32, shape, 0)
    spot = jnp.where(lane == grp * rows + row, jnp.broadcast_to(column, shape), 0.0)
    mine = jnp.sum(spot, axis=0, keepdims=True)
    charge[0] = mine
    pl.semaphore_wait(ready, n - 1)
    charge_copies = []
    for step in reversed(range(regions)):
        for mask in reversed(range(n)):
            if step or mask:
                slot = step * n + mask
                copy = remote(
                    charge.at[0], charge_in.at[slot], qsend.at[slot], qrecv.at[slot],
                    grp=lax.rem(grp + step, regions), dev=me ^ mask,
                )
                copy.start()
                charge_copies.append(copy)
    waved = macc[...]
    sums = []
    for z in range(FZ):
        cos = waved[z * rows : (z + 1) * rows]
        sin = waved[(FZ + z) * rows : (FZ + z + 1) * rows]
        sums.append(cos + half_turn(sin, -1.0, 1.0))
        moments[z] = sums[z]
    moment_copies = []
    for mask in range(1, n):
        copy = remote(
            moments, moments_in.at[mask], tsend.at[mask], trecv.at[mask], dev=me ^ mask
        )
        copy.start()
        moment_copies.append(copy)
    for mask in dict.fromkeys(rounds[-1][1]):
        send_density(mask)
    for copy in moment_copies:
        copy.wait()
    lane, fx, fy = lane_modes((rows, TB))
    first, second = [], []
    for z in range(FZ):
        for mask in range(1, n):
            sums[z] = sums[z] + moments_in[mask, z]
        gain = 0.1 / (1.0 + 0.1 * (fx * fx + fy * fy + float(z * z)))
        value = sums[z] * gain
        first.append(value)
        second.append(half_turn(value, 1.0, -1.0))
    both = stack_split(jnp.concatenate(first + second, axis=0))

    def near_cols(first, count):
        cols = pl.ds(first, count)
        out = table_dot(both, t1h[:, cols], t1l[:, cols], False)
        total = jnp.zeros((rows, count), f32)
        for j in range(WAVES):
            total = total + out[j * rows : (j + 1) * rows] * t2[j : j + 1, cols]
        near_acc[:, cols] = jnp.sum(total * spread[:, cols], axis=0, keepdims=True)

    for q in range(0, n * here, here):
        near_cols(q, here)
    for c in range(parts):
        for b in range(batches):
            turn(rounds[-1][1][b], b, c)
    for copy in density_sends:
        copy.wait()
    rho = part[0]
    for mask in range(1, n):
        rho = rho + part_in[mask]
    density[...] = rho
    for copy in started:
        copy.wait_send()

    for copy in charge_copies:
        copy.wait()
    total = mine
    for slot in range(1, n * regions):
        total = total + charge_in[slot]
    every = regions * rows
    shape = (every, lanes)
    lane = lax.broadcasted_iota(i32, shape, 1)
    row = lax.broadcasted_iota(i32, shape, 0)
    spot = jnp.where(lane == row, jnp.broadcast_to(total, shape), 0.0)
    column = jnp.sum(spot, axis=1, keepdims=True)
    for q in range(0, n * here, here):
        cols = slice(q, q + here)
        field = near_acc[:, cols] + jnp.sum(far[:, cols] * column, axis=0, keepdims=True)
        if q == 0:
            potential[...] = field
        scaled[q // here] = wrow[:, cols] * field


def hamilton_kernel(
    union, meta_v, land, flip, scaled, density8, potential8, out, density, potential,
    meta, result, meta_sem, out_sem, *scratch,
):
    n, batches, held, points = land.shape[:4]
    stored = out.shape[0]
    me = lax.axis_index("dev")
    rights, totals = scratch[:batches], scratch[batches:]
    banks = len(totals)
    fetch = pltpu.make_async_copy(meta_v, meta, meta_sem)
    fetch.start()
    for q in range(density.shape[0]):
        density[q : q + 1, :] = density8[0:1, q * TB : (q + 1) * TB]
        potential[q : q + 1, :] = potential8[0:1, q * TB : (q + 1) * TB]

    def clear(t, carry):
        for total in totals:
            total[t] = jnp.zeros((TB, TB), f32)
        return carry

    def prepare(mask, b):
        line = scaled[mask, :, b * points : (b + 1) * points]
        column = jnp.broadcast_to(line, (TB, points)).T
        for j in range(held):
            rights[b][:, j * TB : (j + 1) * TB] = (column * land[mask, b, j].astype(f32)).astype(bf16)

    def one(mask, carry):
        e = me ^ mask
        for b in range(batches):
            if b + 1 < batches:
                prepare(mask, b + 1)
            else:
                prepare(jnp.minimum(mask + 1, n - 1), 0)
            left = flip[mask, b]
            spots = [meta[e, 1 + b, i] for i in range(held)]
            turn = 0
            for j in range(0, held, 2):
                some = min(2, held - j)
                product = jnp.dot(
                    left, rights[b][:, j * TB : (j + some) * TB], preferred_element_type=f32
                )
                for i in range(held):
                    for t in range(some):
                        slot = meta[e, 0, spots[i] * union + spots[j + t]]
                        tile = product[i * TB : (i + 1) * TB, t * TB : (t + 1) * TB]
                        total = totals[turn % banks]
                        total[slot] = total[slot] + tile
                        turn += 1
        return carry

    lax.fori_loop(0, stored + 1, clear, 0)
    prepare(0, 0)
    fetch.wait()
    lax.fori_loop(0, n, one, 0, unroll=2)

    group = math.gcd(stored, 8)
    copies = []
    for first in range(0, stored, group):
        def finish(t, carry):
            value = totals[0][t]
            for total in totals[1:]:
                value = value + total[t]
            result[t] = value.astype(bf16)
            return carry

        lax.fori_loop(first, first + group, finish, 0)
        at = pl.ds(first, group)
        copy = pltpu.make_async_copy(result.at[at], out.at[at], out_sem.at[first // group])
        copy.start()
        copies.append(copy)
    for copy in copies:
        copy.wait()


def on_device(
    n, regions, orbitals, dens_tiles, point_coords, point_weights, batch_blocks,
    tile_owner, tile_slot, batch_atoms, batch_weights, atom_grid_index,
):
    stored = dens_tiles.shape[0]
    listed = tile_slot.shape[0]
    batches, points, width = orbitals.shape
    here = batches * points
    held = width // TB
    atoms = atom_grid_index.shape[1]
    rows = -(-atoms // 8) * 8
    parts = 2
    banks = 2
    table = (-(-(1 + 3 * batches) // 8) * 8, -(-listed // TB) * TB)
    lanes = -(-regions * rows // TB) * TB
    kept = 4 * n * batches * points * width + 64 * n * here + (1 << 20)
    grant = (62 << 20) - kept
    S = jax.ShapeDtypeStruct
    dma = pltpu.SemaphoreType.DMA
    V = pltpu.VMEM
    density, potential, scaled, meta_all, land, flip = pl.pallas_call(
        functools.partial(region_kernel, n, regions, parts),
        out_shape=(
            V((1, here), f32),
            V((1, here), f32),
            V((n, 1, here), f32),
            V((n, *table), i32),
            V((n, batches, held, points, TB), bf16),
            V((n, batches, width, points), bf16),
        ),
        in_specs=[ANY, VM, VM, VM, VM, VM, VM, VM, ANY, SM],
        out_specs=(VM, VM, VM, VM, VM, VM),
        scratch_shapes=[
            V(table, i32),
            V((n, *table), i32),
            pltpu.SMEM((n, *table), i32),
            V((n, 3, here), f32),
            V((n, 1, here), f32),
            V((stored + 1, TB, TB), bf16),
            V((batches, width, width), bf16),
            V((2 * FXY, n * here), bf16),
            V((2 * FXY, n * here), bf16),
            V((WAVES, n * here), f32),
            V((rows, n * here), f32),
            V((1, n * here), f32),
            V((regions * rows, n * here), f32),
            V((1, WAVES * regions * rows, TB), f32),
            V((regions, FZ, rows, TB), f32),
            V((n, 1, here), f32),
            V((n, 1, here), f32),
            V((WAVES * rows, TB), f32),
            V((FZ, rows, TB), f32),
            V((n, FZ, rows, TB), f32),
            V((1, n * here), f32),
            V((rows, TB), f32),
            V((1, 1, lanes), f32),
            V((n * regions, 1, lanes), f32),
            dma((batches, held)),
            dma((4,)),
            dma((batches, parts, n)), dma((batches, parts, n)),
            dma((3, n)), dma((3, n)),
            dma((regions,)), dma((regions,)),
            dma((n,)), dma((n,)), dma((n,)), dma((n,)),
            dma((n * regions,)), dma((n * regions,)),
            pltpu.SemaphoreType.REGULAR,
        ],
        compiler_params=pltpu.CompilerParams(
            collective_id=0, has_side_effects=True, vmem_limit_bytes=grant
        ),
        name="region",
    )(
        orbitals, tile_owner.reshape(1, listed), tile_slot.reshape(1, listed), batch_blocks,
        batch_atoms, batch_weights, point_coords, point_weights.reshape(1, here), dens_tiles,
        atom_grid_index,
    )
    density, potential, scaled, meta_all, land, flip = [
        pltpu.with_memory_space_constraint(value, pltpu.VMEM)
        for value in (density, potential, scaled, meta_all, land, flip)
    ]
    ham_tiles, density, potential = pl.pallas_call(
        functools.partial(hamilton_kernel, math.isqrt(listed)),
        out_shape=(
            S((stored, TB, TB), bf16), S((here // TB, TB), f32), S((here // TB, TB), f32),
        ),
        in_specs=[VM, VM, VM, VM, VM, VM],
        out_specs=(ANY, VM, VM),
        scratch_shapes=[
            pltpu.SMEM((n, *table), i32),
            V((stored, TB, TB), bf16),
            dma,
            dma((stored // math.gcd(stored, 8),)),
            *[V((points, width), bf16) for _ in range(batches)],
            *[V((stored + 1, TB, TB), f32) for _ in range(banks)],
        ],
        compiler_params=pltpu.CompilerParams(vmem_limit_bytes=grant),
        name="hamilton",
    )(meta_all, land, flip, scaled, density, potential)
    return density.reshape(-1), potential.reshape(-1), ham_tiles


def solution(mesh):
    body = functools.partial(on_device, mesh.shape["dev"], mesh.shape["grp"])
    in_specs = (
        P(("grp", "dev"), None, None),
        P(("grp", "dev"), None, None),
        P(None, ("grp", "dev")),
        P(("grp", "dev")),
        P(("grp", "dev"), None),
        P(("grp", "dev"), None),
        P(("grp", "dev")),
        P(("grp", "dev"), None),
        P(("grp", "dev"), None),
        P(None, "grp"),
    )
    out_specs = (P(("grp", "dev")), P(("grp", "dev")), P(("grp", "dev"), None, None))
    return jax.shard_map(body, mesh=mesh, in_specs=in_specs, out_specs=out_specs, check_vma=False)
```

```python
import functools
import math

import jax
import jax.numpy as jnp
from jax import lax
from jax.experimental import pallas as pl
from jax.experimental.pallas import tpu as pltpu
from jax.sharding import PartitionSpec as P

TB = 128
KM = 512
GRIDN = 64
FXY = 64
FZ = KM // 2 // FXY
WAVES = 2 * FZ
MESH = pl.DeviceIdType.MESH
VM = pl.BlockSpec(memory_space=pltpu.VMEM)
SM = pl.BlockSpec(memory_space=pltpu.SMEM)
ANY = pl.BlockSpec(memory_space=pl.ANY)
f32, i32, bf16 = jnp.float32, jnp.int32, jnp.bfloat16


def turn_trig(turns):
    angle = (turns - jnp.round(turns)) * (2.0 * math.pi)
    return jnp.cos(angle), jnp.sin(angle)


def stack_split(value):
    high = value.astype(bf16)
    rest = (value - high.astype(f32)).astype(bf16)
    return jnp.concatenate([high, rest], axis=0)


def table_dot(both, high, low, turned):
    rows = both.shape[0] // 2
    dims = (((1,), (1 if turned else 0,)), ((), ()))
    out = lax.dot_general(both, high, dims, preferred_element_type=f32)
    fine = lax.dot_general(both[:rows], low, dims, preferred_element_type=f32)
    return out[:rows] + out[rows:] + fine


def lane_modes(shape):
    lane = lax.broadcasted_iota(i32, shape, 1)
    fx = (lane & 7).astype(f32)
    fy = ((lane >> 3) & 7).astype(f32)
    return lane, fx, fy


def half_turn(value, first, second):
    lane = lax.broadcasted_iota(i32, value.shape, 1)
    return pltpu.roll(value, FXY, 1) * jnp.where(lane < FXY, first, second)


def region_kernel(
    n, regions, parts, orb, owner, slot, blocks, batch_atoms, batch_weights, coords, weights,
    dens, grid_s,
    density, potential, scaled, meta_all, land, flip,
    facts, meta_v, meta_s, coords_all, weights_all, tiles, block,
    t1h, t1l, t2, spread, wrow, far, lhs_far, waves, part, part_in,
    macc, moments, moments_in, near_acc, qacc, charge, charge_in,
    pack_sem, local_sem, send, recv, fsend, frecv, wsend, wrecv,
    dsend, drecv, tsend, trecv, qsend, qrecv, ready,
):
    me = lax.axis_index("dev")
    grp = lax.axis_index("grp")
    bits = n.bit_length() - 1
    batches, points, width = orb.shape
    here = batches * points
    held = width // TB
    stored = dens.shape[0]
    atoms = grid_s.shape[1]
    rows = spread.shape[0]
    piece = points // parts
    lanes = charge.shape[2]
    listed = owner.shape[1]
    near = batch_atoms.shape[1]
    union = math.isqrt(listed)
    block_at, atom_at, weight_at = 1, 1 + batches, 1 + 2 * batches

    barrier = pltpu.get_barrier_semaphore()
    for mask in range(1, n):
        pl.semaphore_signal(barrier, inc=1, device_id={"dev": me ^ mask}, device_id_type=MESH)
    for step in range(1, regions):
        pl.semaphore_signal(
            barrier, inc=1, device_id={"grp": lax.rem(grp + step, regions)}, device_id_type=MESH
        )
    packs = []
    for b in range(batches):
        for u in range(held):
            copy = pltpu.make_async_copy(
                orb.at[b, :, pl.ds(u * TB, TB)], land.at[0, b, u], pack_sem.at[b, u]
            )
            copy.start()
            packs.append(copy)
    own = [pltpu.make_async_copy(dens, tiles.at[pl.ds(0, stored)], local_sem.at[0])]
    own[0].start()
    facts[...] = jnp.zeros_like(facts)
    facts[0:1, 0:listed] = owner[...] * stored + slot[...]
    facts[block_at : block_at + batches, 0:held] = blocks[...]
    facts[atom_at : atom_at + batches, 0:near] = batch_atoms[...]
    facts[weight_at : weight_at + batches, 0:near] = batch_weights[...]
    tiles[stored] = jnp.zeros((TB, TB), bf16)
    macc[...] = jnp.zeros_like(macc)
    qacc[...] = jnp.zeros_like(qacc)
    for copy in packs:
        copy.wait()
    pl.semaphore_wait(barrier, n + regions - 2)

    def remote(src, dst, ssem, rsem, **where):
        return pltpu.make_async_remote_copy(
            src_ref=src, dst_ref=dst, send_sem=ssem, recv_sem=rsem,
            device_id=where, device_id_type=MESH,
        )

    def order_of(b):
        return list(range(bits)) if b % 2 == 0 else list(range(bits))[::-1]

    def landing(mask, b, c):
        return land.at[mask, b, :, pl.ds(c * piece, piece), :]

    def orb_copy(b, stage, mask, c):
        bit = 1 << order_of(b)[stage]
        got = mask ^ bit
        return remote(
            landing(mask, b, c), landing(got, b, c), send.at[b, c, got], recv.at[b, c, got],
            dev=me ^ bit,
        )

    started = []
    feats = []
    pairs = ((facts, meta_v), (coords, coords_all), (weights, weights_all))
    for mask in range(1, n):
        for k, (src, dst) in enumerate(pairs):
            copy = remote(src, dst.at[me], fsend.at[k, mask], frecv.at[k, mask], dev=me ^ mask)
            copy.start()
            feats.append(copy)
    for stage in range(bits):
        for b in range(batches):
            for c in range(parts):
                copy = orb_copy(b, stage, 0, c)
                copy.start()
                started.append(copy)
    for k, (src, dst) in enumerate(pairs, 1):
        copy = pltpu.make_async_copy(src, dst.at[me], local_sem.at[k])
        copy.start()
        own.append(copy)
    for mask in range(1, n):
        pl.semaphore_signal(ready, inc=1, device_id={"dev": me ^ mask}, device_id_type=MESH)

    shape = (rows, TB)
    lane, fx, fy = lane_modes(shape)
    row = lax.broadcasted_iota(i32, shape, 0)
    place = []
    for c in range(3):
        at = jnp.zeros(shape, f32)
        for a in range(atoms):
            at = jnp.where(row == a, grid_s[c, a].astype(f32), at)
        place.append(at)
    for z in range(FZ):
        turns = (fx * place[0] + fy * place[1] + place[2] * float(z)) * (1.0 / GRIDN)
        cos, sin = turn_trig(turns)
        gain = 0.03 / (1.0 + 0.1 * (fx * fx + fy * fy + float(z * z)))
        wave = jnp.where(lane < FXY, cos, sin) * gain
        waves[grp, z] = jnp.where(row < atoms, wave, 0.0)
    wave_copies = []
    for step in range(1, regions):
        copy = remote(
            waves.at[grp], waves.at[grp], wsend.at[step], wrecv.at[step],
            grp=lax.rem(grp + step, regions),
        )
        copy.start()
        wave_copies.append(copy)

    for copy in feats + own:
        copy.wait()
    codes = meta_v[...]
    at = lax.broadcasted_iota(i32, codes.shape, 1)
    local = codes - me * stored
    mine = (local >= 0) & (local < stored)
    meta_all[...] = jnp.where(at == 0, jnp.where(mine, local, stored), codes)
    moved = [pltpu.make_async_copy(meta_all, meta_s, local_sem.at[0])]
    for copy in moved:
        copy.start()

    def mask_cols(mask, first, count):
        return pl.ds(pl.multiple_of(mask * here + first, TB), count)

    def tables(mask, carry):
        e = me ^ mask
        cols = mask_cols(mask, 0, here)
        step = lax.broadcasted_iota(i32, (8, here), 0)
        where = coords_all[e]
        first = []
        for c in range(2):
            turns = step.astype(f32) * where[c : c + 1, :] * (1.0 / GRIDN)
            first.append(turn_trig(turns))
        (cx, sx), (cy, sy) = first
        for y in range(0, 8, 2):
            cos, sin = [], []
            for q in (y, y + 1):
                cq, sq = cy[q : q + 1, :], sy[q : q + 1, :]
                cos.append(cx * cq - sx * sq)
                sin.append(sx * cq + cx * sq)
            for base, wave in ((0, cos), (FXY, sin)):
                wave = jnp.concatenate(wave, axis=0)
                high = wave.astype(bf16)
                t1h[base + y * 8 : base + y * 8 + 16, cols] = high
                t1l[base + y * 8 : base + y * 8 + 16, cols] = (wave - high.astype(f32)).astype(bf16)
        step = lax.broadcasted_iota(i32, (WAVES, here), 0)
        times = jnp.where(step < FZ, step, step - FZ).astype(f32)
        cz, sz = turn_trig(times * where[2:3, :] * (1.0 / GRIDN))
        t2[:, cols] = jnp.where(step < FZ, cz, sz)
        wrow[:, cols] = weights_all[e]
        row = lax.broadcasted_iota(i32, (rows, points), 0)
        for b in range(batches):
            total = jnp.int32(0)
            for k in range(near):
                total = total + meta_s[e, weight_at + b, k]
            share = jnp.zeros((rows, points), i32)
            spot = [jnp.zeros((rows, points), f32) for c in range(3)]
            for a in range(atoms):
                part_of = jnp.int32(0)
                for k in range(near):
                    weight = meta_s[e, weight_at + b, k]
                    part_of = part_of + jnp.where(
                        meta_s[e, atom_at + b, k] == a, weight, 0
                    )
                share = jnp.where(row == a, part_of, share)
                for c in range(3):
                    spot[c] = jnp.where(row == a, grid_s[c, a].astype(f32), spot[c])
            squared = jnp.zeros((rows, points), f32)
            for c in range(3):
                gone = where[c : c + 1, b * points : (b + 1) * points] - spot[c]
                squared = squared + gone * gone
            fraction = share.astype(f32) / jnp.full((rows, points), total.astype(f32))
            spread[:, mask_cols(mask, b * points, points)] = fraction * jnp.exp(
                squared * (-2.0 / (GRIDN * GRIDN))
            )
        return carry

    def far_rows():
        for z in range(FZ):
            for g in range(regions):
                cs = waves[g, z]
                for j, value in ((z, cs), (FZ + z, half_turn(cs, 1.0, -1.0))):
                    first = (j * regions + g) * rows
                    lhs_far[0, first : first + rows, :] = value
        return None

    def far_cols(q, carry):
        cols = pl.ds(pl.multiple_of(q * 2 * TB, 2 * TB), 2 * TB)
        high, low = t1h[:, cols], t1l[:, cols]
        every = regions * rows
        total = jnp.zeros((every, 2 * TB), f32)
        for j in range(WAVES):
            value = lhs_far[0, j * every : (j + 1) * every, :]
            out = table_dot(stack_split(value), high, low, False)
            total = total + out * t2[j : j + 1, cols]
        far[:, cols] = total
        return carry

    def assemble(mask, b):
        e = me ^ mask

        def block_row(i, carry):
            first = meta_s[e, block_at + b, i] * union
            for j in range(held):
                index = meta_s[e, 0, first + meta_s[e, block_at + b, j]]
                block[b, pl.ds(pl.multiple_of(i * TB, TB), TB), j * TB : (j + 1) * TB] = tiles[index]
            return carry

        lax.fori_loop(0, held, block_row, 0)

    def process(mask, b, c):
        at = slice(c * piece, (c + 1) * piece)
        cols = slice(mask * here + b * points + c * piece, mask * here + b * points + (c + 1) * piece)
        orbital = [land[mask, b, u, at, :] for u in range(held)]
        lhs = jnp.concatenate(orbital, axis=1)
        total = jnp.zeros((piece, TB), f32)
        for v in range(0, held, 2):
            some = min(2, held - v)
            product = jnp.dot(lhs, block[b, :, v * TB : (v + some) * TB], preferred_element_type=f32)
            for t in range(some):
                total = total + product[:, t * TB : (t + 1) * TB] * orbital[v + t].astype(f32)
        line = jnp.sum(total.T, axis=0, keepdims=True)
        part[mask, :, b * points + c * piece : b * points + (c + 1) * piece] = line
        source = spread[:, cols] * (wrow[:, cols] * line)
        folded = source[:, 0:TB]
        for q in range(TB, piece, TB):
            folded = folded + source[:, q : q + TB]
        qacc[...] = qacc[...] + folded
        return source, cols

    def gather(source, cols):
        waved = jnp.concatenate([source * t2[j : j + 1, cols] for j in range(WAVES)], axis=0)
        macc[...] = macc[...] + table_dot(stack_split(waved), t1h[:, cols], t1l[:, cols], True)

    def turn(mask, b, c):
        at = slice(c * piece, (c + 1) * piece)
        for u in range(held):
            flip[mask, b, u * TB : (u + 1) * TB, at] = land[mask, b, u, at, :].T

    density_sends = []

    def send_density(mask):
        if mask:
            copy = remote(
                part.at[mask], part_in.at[mask], dsend.at[mask], drecv.at[mask], dev=me ^ mask
            )
            copy.start()
            density_sends.append(copy)

    rounds = [(None, [0] * batches)]
    for stage in range(bits):
        for low in range(1 << stage):
            masks = []
            for b in range(batches):
                got = 1 << order_of(b)[stage]
                for t in range(stage):
                    if low >> t & 1:
                        got ^= 1 << order_of(b)[t]
                masks.append(got)
            rounds.append((stage, masks))
    done = {}
    for copy in moved:
        copy.wait()
    lax.fori_loop(0, n, tables, 0)
    for number, (stage, masks) in enumerate(rounds):
        last = number == len(rounds) - 1
        for b in range(batches):
            assemble(masks[b], b)
        if last:
            for copy in wave_copies:
                copy.wait()
            far_rows()
            lax.fori_loop(0, n * here // (2 * TB), far_cols, 0)
        for c in range(parts):
            for b in range(batches):
                mask = masks[b]
                if stage is not None:
                    there = landing(mask, b, c)
                    bit = 1 << order_of(b)[stage]
                    remote(
                        there, there, send.at[b, c, mask], recv.at[b, c, mask], dev=me ^ bit
                    ).wait_recv()
                    for later in range(stage + 1, bits):
                        copy = orb_copy(b, later, mask, c)
                        copy.start()
                        started.append(copy)
            sources = [process(masks[b], b, c) for b in range(batches)]
            if not (last and c == parts - 1):
                for source in sources:
                    gather(*source)
            if not last:
                for b in range(batches):
                    turn(masks[b], b, c)
        for mask in masks:
            done[mask] = done.get(mask, 0) + 1
            if done[mask] == batches and not last:
                send_density(mask)

    column = jnp.sum(qacc[...], axis=1, keepdims=True)
    shape = (rows, lanes)
    lane = lax.broadcasted_iota(i32, shape, 1)
    row = lax.broadcasted_iota(i32, shape, 0)
    spot = jnp.where(lane == grp * rows + row, jnp.broadcast_to(column, shape), 0.0)
    mine = jnp.sum(spot, axis=0, keepdims=True)
    charge[0] = mine
    pl.semaphore_wait(ready, n - 1)
    charge_copies = []
    for step in reversed(range(regions)):
        for mask in reversed(range(n)):
            if step or mask:
                slot = step * n + mask
                copy = remote(
                    charge.at[0], charge_in.at[slot], qsend.at[slot], qrecv.at[slot],
                    grp=lax.rem(grp + step, regions), dev=me ^ mask,
                )
                copy.start()
                charge_copies.append(copy)
    for source in sources:
        gather(*source)
    waved = macc[...]
    sums = []
    for z in range(FZ):
        cos = waved[z * rows : (z + 1) * rows]
        sin = waved[(FZ + z) * rows : (FZ + z + 1) * rows]
        sums.append(cos + half_turn(sin, -1.0, 1.0))
        moments[z] = sums[z]
    moment_copies = []
    for mask in range(1, n):
        copy = remote(
            moments, moments_in.at[mask], tsend.at[mask], trecv.at[mask], dev=me ^ mask
        )
        copy.start()
        moment_copies.append(copy)
    for mask in dict.fromkeys(rounds[-1][1]):
        send_density(mask)
    for c in range(parts):
        for b in range(batches):
            turn(rounds[-1][1][b], b, c)
    for copy in moment_copies:
        copy.wait()
    lane, fx, fy = lane_modes((rows, TB))
    first, second = [], []
    for z in range(FZ):
        for mask in range(1, n):
            sums[z] = sums[z] + moments_in[mask, z]
        gain = 0.1 / (1.0 + 0.1 * (fx * fx + fy * fy + float(z * z)))
        value = sums[z] * gain
        first.append(value)
        second.append(half_turn(value, 1.0, -1.0))
    both = stack_split(jnp.concatenate(first + second, axis=0))

    def near_cols(first, count):
        cols = pl.ds(first, count)
        out = table_dot(both, t1h[:, cols], t1l[:, cols], False)
        total = jnp.zeros((rows, count), f32)
        for j in range(WAVES):
            total = total + out[j * rows : (j + 1) * rows] * t2[j : j + 1, cols]
        near_acc[:, cols] = jnp.sum(total * spread[:, cols], axis=0, keepdims=True)

    for q in range(0, n * here, here):
        near_cols(q, here)
    for copy in density_sends:
        copy.wait()
    rho = part[0]
    for mask in range(1, n):
        rho = rho + part_in[mask]
    density[...] = rho
    for copy in started:
        copy.wait_send()

    for copy in charge_copies:
        copy.wait()
    total = mine
    for slot in range(1, n * regions):
        total = total + charge_in[slot]
    every = regions * rows
    shape = (every, lanes)
    lane = lax.broadcasted_iota(i32, shape, 1)
    row = lax.broadcasted_iota(i32, shape, 0)
    spot = jnp.where(lane == row, jnp.broadcast_to(total, shape), 0.0)
    column = jnp.sum(spot, axis=1, keepdims=True)
    for q in range(0, n * here, here):
        cols = slice(q, q + here)
        field = near_acc[:, cols] + jnp.sum(far[:, cols] * column, axis=0, keepdims=True)
        if q == 0:
            potential[...] = field
        scaled[q // here] = wrow[:, cols] * field


def hamilton_kernel(
    union, meta_v, land, flip, scaled, density8, potential8, out, density, potential,
    meta, result, meta_sem, out_sem, *scratch,
):
    n, batches, held, points = land.shape[:4]
    stored = out.shape[0]
    me = lax.axis_index("dev")
    rights, totals = scratch[:batches], scratch[batches:]
    banks = len(totals)
    fetch = pltpu.make_async_copy(meta_v, meta, meta_sem)
    fetch.start()
    for q in range(density.shape[0]):
        density[q : q + 1, :] = density8[0:1, q * TB : (q + 1) * TB]
        potential[q : q + 1, :] = potential8[0:1, q * TB : (q + 1) * TB]

    def clear(t, carry):
        for total in totals:
            total[t] = jnp.zeros((TB, TB), f32)
        return carry

    def prepare(mask, b):
        line = scaled[mask, :, b * points : (b + 1) * points]
        column = jnp.broadcast_to(line, (TB, points)).T
        for j in range(held):
            rights[b][:, j * TB : (j + 1) * TB] = (column * land[mask, b, j].astype(f32)).astype(bf16)

    def one(mask, carry):
        e = me ^ mask
        for b in range(batches):
            if b + 1 < batches:
                prepare(mask, b + 1)
            else:
                prepare(jnp.minimum(mask + 1, n - 1), 0)
            left = flip[mask, b]
            spots = [meta[e, 1 + b, i] for i in range(held)]
            turn = 0
            for j in range(0, held, 2):
                some = min(2, held - j)
                product = jnp.dot(
                    left, rights[b][:, j * TB : (j + some) * TB], preferred_element_type=f32
                )
                for i in range(held):
                    for t in range(some):
                        slot = meta[e, 0, spots[i] * union + spots[j + t]]
                        tile = product[i * TB : (i + 1) * TB, t * TB : (t + 1) * TB]
                        total = totals[turn % banks]
                        total[slot] = total[slot] + tile
                        turn += 1
        return carry

    lax.fori_loop(0, stored + 1, clear, 0)
    prepare(0, 0)
    fetch.wait()
    lax.fori_loop(0, n, one, 0, unroll=2)

    group = math.gcd(stored, 8)
    copies = []
    for first in range(0, stored, group):
        def finish(t, carry):
            value = totals[0][t]
            for total in totals[1:]:
                value = value + total[t]
            result[t] = value.astype(bf16)
            return carry

        lax.fori_loop(first, first + group, finish, 0)
        at = pl.ds(first, group)
        copy = pltpu.make_async_copy(result.at[at], out.at[at], out_sem.at[first // group])
        copy.start()
        copies.append(copy)
    for copy in copies:
        copy.wait()


def on_device(
    n, regions, orbitals, dens_tiles, point_coords, point_weights, batch_blocks,
    tile_owner, tile_slot, batch_atoms, batch_weights, atom_grid_index,
):
    stored = dens_tiles.shape[0]
    listed = tile_slot.shape[0]
    batches, points, width = orbitals.shape
    here = batches * points
    held = width // TB
    atoms = atom_grid_index.shape[1]
    rows = -(-atoms // 8) * 8
    parts = 2
    banks = 2
    table = (-(-(1 + 3 * batches) // 8) * 8, -(-listed // TB) * TB)
    lanes = -(-regions * rows // TB) * TB
    kept = 4 * n * batches * points * width + 64 * n * here + (1 << 20)
    grant = (62 << 20) - kept
    S = jax.ShapeDtypeStruct
    dma = pltpu.SemaphoreType.DMA
    V = pltpu.VMEM
    density, potential, scaled, meta_all, land, flip = pl.pallas_call(
        functools.partial(region_kernel, n, regions, parts),
        out_shape=(
            V((1, here), f32),
            V((1, here), f32),
            V((n, 1, here), f32),
            V((n, *table), i32),
            V((n, batches, held, points, TB), bf16),
            V((n, batches, width, points), bf16),
        ),
        in_specs=[ANY, VM, VM, VM, VM, VM, VM, VM, ANY, SM],
        out_specs=(VM, VM, VM, VM, VM, VM),
        scratch_shapes=[
            V(table, i32),
            V((n, *table), i32),
            pltpu.SMEM((n, *table), i32),
            V((n, 3, here), f32),
            V((n, 1, here), f32),
            V((stored + 1, TB, TB), bf16),
            V((batches, width, width), bf16),
            V((2 * FXY, n * here), bf16),
            V((2 * FXY, n * here), bf16),
            V((WAVES, n * here), f32),
            V((rows, n * here), f32),
            V((1, n * here), f32),
            V((regions * rows, n * here), f32),
            V((1, WAVES * regions * rows, TB), f32),
            V((regions, FZ, rows, TB), f32),
            V((n, 1, here), f32),
            V((n, 1, here), f32),
            V((WAVES * rows, TB), f32),
            V((FZ, rows, TB), f32),
            V((n, FZ, rows, TB), f32),
            V((1, n * here), f32),
            V((rows, TB), f32),
            V((1, 1, lanes), f32),
            V((n * regions, 1, lanes), f32),
            dma((batches, held)),
            dma((4,)),
            dma((batches, parts, n)), dma((batches, parts, n)),
            dma((3, n)), dma((3, n)),
            dma((regions,)), dma((regions,)),
            dma((n,)), dma((n,)), dma((n,)), dma((n,)),
            dma((n * regions,)), dma((n * regions,)),
            pltpu.SemaphoreType.REGULAR,
        ],
        compiler_params=pltpu.CompilerParams(
            collective_id=0, has_side_effects=True, vmem_limit_bytes=grant
        ),
        name="region",
    )(
        orbitals, tile_owner.reshape(1, listed), tile_slot.reshape(1, listed), batch_blocks,
        batch_atoms, batch_weights, point_coords, point_weights.reshape(1, here), dens_tiles,
        atom_grid_index,
    )
    density, potential, scaled, meta_all, land, flip = [
        pltpu.with_memory_space_constraint(value, pltpu.VMEM)
        for value in (density, potential, scaled, meta_all, land, flip)
    ]
    ham_tiles, density, potential = pl.pallas_call(
        functools.partial(hamilton_kernel, math.isqrt(listed)),
        out_shape=(
            S((stored, TB, TB), bf16), S((here // TB, TB), f32), S((here // TB, TB), f32),
        ),
        in_specs=[VM, VM, VM, VM, VM, VM],
        out_specs=(ANY, VM, VM),
        scratch_shapes=[
            pltpu.SMEM((n, *table), i32),
            V((stored, TB, TB), bf16),
            dma,
            dma((stored // math.gcd(stored, 8),)),
            *[V((points, width), bf16) for _ in range(batches)],
            *[V((stored + 1, TB, TB), f32) for _ in range(banks)],
        ],
        compiler_params=pltpu.CompilerParams(vmem_limit_bytes=grant),
        name="hamilton",
    )(meta_all, land, flip, scaled, density, potential)
    return density.reshape(-1), potential.reshape(-1), ham_tiles


def solution(mesh):
    body = functools.partial(on_device, mesh.shape["dev"], mesh.shape["grp"])
    in_specs = (
        P(("grp", "dev"), None, None),
        P(("grp", "dev"), None, None),
        P(None, ("grp", "dev")),
        P(("grp", "dev")),
        P(("grp", "dev"), None),
        P(("grp", "dev"), None),
        P(("grp", "dev")),
        P(("grp", "dev"), None),
        P(("grp", "dev"), None),
        P(None, "grp"),
    )
    out_specs = (P(("grp", "dev")), P(("grp", "dev")), P(("grp", "dev"), None, None))
    return jax.shard_map(body, mesh=mesh, in_specs=in_specs, out_specs=out_specs, check_vma=False)
```

```python
import functools
import math

import jax
import jax.numpy as jnp
from jax import lax
from jax.experimental import pallas as pl
from jax.experimental.pallas import tpu as pltpu
from jax.sharding import PartitionSpec as P

TB = 128
KM = 512
GRIDN = 64
FXY = 64
FZ = KM // 2 // FXY
WAVES = 2 * FZ
MESH = pl.DeviceIdType.MESH
VM = pl.BlockSpec(memory_space=pltpu.VMEM)
SM = pl.BlockSpec(memory_space=pltpu.SMEM)
ANY = pl.BlockSpec(memory_space=pl.ANY)
f32, i32, bf16 = jnp.float32, jnp.int32, jnp.bfloat16


def turn_trig(turns):
    angle = (turns - jnp.round(turns)) * (2.0 * math.pi)
    return jnp.cos(angle), jnp.sin(angle)


def stack_split(value):
    high = value.astype(bf16)
    rest = (value - high.astype(f32)).astype(bf16)
    return jnp.concatenate([high, rest], axis=0)


def table_dot(both, high, low, turned):
    rows = both.shape[0] // 2
    dims = (((1,), (1 if turned else 0,)), ((), ()))
    out = lax.dot_general(both, high, dims, preferred_element_type=f32)
    fine = lax.dot_general(both[:rows], low, dims, preferred_element_type=f32)
    return out[:rows] + out[rows:] + fine


def lane_modes(shape):
    lane = lax.broadcasted_iota(i32, shape, 1)
    fx = (lane & 7).astype(f32)
    fy = ((lane >> 3) & 7).astype(f32)
    return lane, fx, fy


def half_turn(value, first, second):
    lane = lax.broadcasted_iota(i32, value.shape, 1)
    return pltpu.roll(value, FXY, 1) * jnp.where(lane < FXY, first, second)


def region_kernel(
    n, regions, parts, orb, owner, slot, blocks, batch_atoms, batch_weights, coords, weights,
    dens, grid_s,
    density, potential, scaled, meta_all, land, flip,
    facts, meta_v, meta_s, coords_all, weights_all, tiles, block,
    t1h, t1l, t2, spread, wrow, far, lhs_far, waves, part, part_in,
    macc, moments, moments_in, near_acc, qacc, charge, charge_in,
    pack_sem, local_sem, send, recv, fsend, frecv, wsend, wrecv,
    dsend, drecv, tsend, trecv, qsend, qrecv, ready,
):
    me = lax.axis_index("dev")
    grp = lax.axis_index("grp")
    bits = n.bit_length() - 1
    batches, points, width = orb.shape
    here = batches * points
    held = width // TB
    stored = dens.shape[0]
    atoms = grid_s.shape[1]
    rows = spread.shape[0]
    piece = points // parts
    lanes = charge.shape[2]
    listed = owner.shape[1]
    near = batch_atoms.shape[1]
    union = math.isqrt(listed)
    block_at, atom_at, weight_at = 1, 1 + batches, 1 + 2 * batches

    barrier = pltpu.get_barrier_semaphore()
    for mask in range(1, n):
        pl.semaphore_signal(barrier, inc=1, device_id={"dev": me ^ mask}, device_id_type=MESH)
    for step in range(1, regions):
        pl.semaphore_signal(
            barrier, inc=1, device_id={"grp": lax.rem(grp + step, regions)}, device_id_type=MESH
        )
    packs = []
    for b in range(batches):
        for u in range(held):
            copy = pltpu.make_async_copy(
                orb.at[b, :, pl.ds(u * TB, TB)], land.at[0, b, u], pack_sem.at[b, u]
            )
            copy.start()
            packs.append(copy)
    own = [pltpu.make_async_copy(dens, tiles.at[pl.ds(0, stored)], local_sem.at[0])]
    own[0].start()
    facts[...] = jnp.zeros_like(facts)
    facts[0:1, 0:listed] = owner[...] * stored + slot[...]
    facts[block_at : block_at + batches, 0:held] = blocks[...]
    facts[atom_at : atom_at + batches, 0:near] = batch_atoms[...]
    facts[weight_at : weight_at + batches, 0:near] = batch_weights[...]
    tiles[stored] = jnp.zeros((TB, TB), bf16)
    macc[...] = jnp.zeros_like(macc)
    qacc[...] = jnp.zeros_like(qacc)
    for copy in packs:
        copy.wait()
    pl.semaphore_wait(barrier, n + regions - 2)

    def remote(src, dst, ssem, rsem, **where):
        return pltpu.make_async_remote_copy(
            src_ref=src, dst_ref=dst, send_sem=ssem, recv_sem=rsem,
            device_id=where, device_id_type=MESH,
        )

    def order_of(b):
        return list(range(bits)) if b % 2 == 0 else list(range(bits))[::-1]

    def landing(mask, b, c):
        return land.at[mask, b, :, pl.ds(c * piece, piece), :]

    def orb_copy(b, stage, mask, c):
        bit = 1 << order_of(b)[stage]
        got = mask ^ bit
        return remote(
            landing(mask, b, c), landing(got, b, c), send.at[b, c, got], recv.at[b, c, got],
            dev=me ^ bit,
        )

    started = []
    feats = []
    pairs = ((facts, meta_v), (coords, coords_all), (weights, weights_all))
    for mask in range(1, n):
        for k, (src, dst) in enumerate(pairs):
            copy = remote(src, dst.at[me], fsend.at[k, mask], frecv.at[k, mask], dev=me ^ mask)
            copy.start()
            feats.append(copy)
    for stage in range(bits):
        for b in range(batches):
            for c in range(parts):
                copy = orb_copy(b, stage, 0, c)
                copy.start()
                started.append(copy)
    for k, (src, dst) in enumerate(pairs, 1):
        copy = pltpu.make_async_copy(src, dst.at[me], local_sem.at[k])
        copy.start()
        own.append(copy)
    for mask in range(1, n):
        pl.semaphore_signal(ready, inc=1, device_id={"dev": me ^ mask}, device_id_type=MESH)

    shape = (rows, TB)
    lane, fx, fy = lane_modes(shape)
    row = lax.broadcasted_iota(i32, shape, 0)
    place = []
    for c in range(3):
        at = jnp.zeros(shape, f32)
        for a in range(atoms):
            at = jnp.where(row == a, grid_s[c, a].astype(f32), at)
        place.append(at)
    for z in range(FZ):
        turns = (fx * place[0] + fy * place[1] + place[2] * float(z)) * (1.0 / GRIDN)
        cos, sin = turn_trig(turns)
        gain = 0.03 / (1.0 + 0.1 * (fx * fx + fy * fy + float(z * z)))
        wave = jnp.where(lane < FXY, cos, sin) * gain
        waves[grp, z] = jnp.where(row < atoms, wave, 0.0)
    wave_copies = []
    for step in range(1, regions):
        copy = remote(
            waves.at[grp], waves.at[grp], wsend.at[step], wrecv.at[step],
            grp=lax.rem(grp + step, regions),
        )
        copy.start()
        wave_copies.append(copy)

    for copy in feats + own:
        copy.wait()
    codes = meta_v[...]
    at = lax.broadcasted_iota(i32, codes.shape, 1)
    local = codes - me * stored
    mine = (local >= 0) & (local < stored)
    meta_all[...] = jnp.where(at == 0, jnp.where(mine, local, stored), codes)
    moved = [pltpu.make_async_copy(meta_all, meta_s, local_sem.at[0])]
    for copy in moved:
        copy.start()

    def mask_cols(mask, first, count):
        return pl.ds(pl.multiple_of(mask * here + first, TB), count)

    def tables(mask, carry):
        e = me ^ mask
        cols = mask_cols(mask, 0, here)
        step = lax.broadcasted_iota(i32, (8, here), 0)
        where = coords_all[e]
        first = []
        for c in range(2):
            turns = step.astype(f32) * where[c : c + 1, :] * (1.0 / GRIDN)
            first.append(turn_trig(turns))
        (cx, sx), (cy, sy) = first
        for y in range(0, 8, 2):
            cos, sin = [], []
            for q in (y, y + 1):
                cq, sq = cy[q : q + 1, :], sy[q : q + 1, :]
                cos.append(cx * cq - sx * sq)
                sin.append(sx * cq + cx * sq)
            for base, wave in ((0, cos), (FXY, sin)):
                wave = jnp.concatenate(wave, axis=0)
                high = wave.astype(bf16)
                t1h[base + y * 8 : base + y * 8 + 16, cols] = high
                t1l[base + y * 8 : base + y * 8 + 16, cols] = (wave - high.astype(f32)).astype(bf16)
        step = lax.broadcasted_iota(i32, (WAVES, here), 0)
        times = jnp.where(step < FZ, step, step - FZ).astype(f32)
        cz, sz = turn_trig(times * where[2:3, :] * (1.0 / GRIDN))
        t2[:, cols] = jnp.where(step < FZ, cz, sz)
        wrow[:, cols] = weights_all[e]
        row = lax.broadcasted_iota(i32, (rows, points), 0)
        for b in range(batches):
            total = jnp.int32(0)
            for k in range(near):
                total = total + meta_s[e, weight_at + b, k]
            share = jnp.zeros((rows, points), i32)
            spot = [jnp.zeros((rows, points), f32) for c in range(3)]
            for a in range(atoms):
                part_of = jnp.int32(0)
                for k in range(near):
                    weight = meta_s[e, weight_at + b, k]
                    part_of = part_of + jnp.where(
                        meta_s[e, atom_at + b, k] == a, weight, 0
                    )
                share = jnp.where(row == a, part_of, share)
                for c in range(3):
                    spot[c] = jnp.where(row == a, grid_s[c, a].astype(f32), spot[c])
            squared = jnp.zeros((rows, points), f32)
            for c in range(3):
                gone = where[c : c + 1, b * points : (b + 1) * points] - spot[c]
                squared = squared + gone * gone
            fraction = share.astype(f32) / jnp.full((rows, points), total.astype(f32))
            spread[:, mask_cols(mask, b * points, points)] = fraction * jnp.exp(
                squared * (-2.0 / (GRIDN * GRIDN))
            )
        return carry

    def far_rows():
        for z in range(FZ):
            for g in range(regions):
                cs = waves[g, z]
                for j, value in ((z, cs), (FZ + z, half_turn(cs, 1.0, -1.0))):
                    first = (j * regions + g) * rows
                    lhs_far[0, first : first + rows, :] = value
        return None

    def far_cols(q, carry):
        cols = pl.ds(pl.multiple_of(q * 2 * TB, 2 * TB), 2 * TB)
        high, low = t1h[:, cols], t1l[:, cols]
        every = regions * rows
        total = jnp.zeros((every, 2 * TB), f32)
        for j in range(WAVES):
            value = lhs_far[0, j * every : (j + 1) * every, :]
            out = table_dot(stack_split(value), high, low, False)
            total = total + out * t2[j : j + 1, cols]
        far[:, cols] = total
        return carry

    def assemble(mask, b):
        e = me ^ mask

        def block_row(i, carry):
            first = meta_s[e, block_at + b, i] * union
            for j in range(held):
                index = meta_s[e, 0, first + meta_s[e, block_at + b, j]]
                block[b, pl.ds(pl.multiple_of(i * TB, TB), TB), j * TB : (j + 1) * TB] = tiles[index]
            return carry

        lax.fori_loop(0, held, block_row, 0)

    def process(mask, b, c):
        at = slice(c * piece, (c + 1) * piece)
        cols = slice(mask * here + b * points + c * piece, mask * here + b * points + (c + 1) * piece)
        orbital = [land[mask, b, u, at, :] for u in range(held)]
        lhs = jnp.concatenate(orbital, axis=1)
        total = jnp.zeros((piece, TB), f32)
        for v in range(0, held, 2):
            some = min(2, held - v)
            product = jnp.dot(lhs, block[b, :, v * TB : (v + some) * TB], preferred_element_type=f32)
            for t in range(some):
                total = total + product[:, t * TB : (t + 1) * TB] * orbital[v + t].astype(f32)
        line = jnp.sum(total.T, axis=0, keepdims=True)
        part[mask, :, b * points + c * piece : b * points + (c + 1) * piece] = line
        source = spread[:, cols] * (wrow[:, cols] * line)
        folded = source[:, 0:TB]
        for q in range(TB, piece, TB):
            folded = folded + source[:, q : q + TB]
        qacc[...] = qacc[...] + folded
        return source, cols

    def gather(source, cols):
        waved = jnp.concatenate([source * t2[j : j + 1, cols] for j in range(WAVES)], axis=0)
        macc[...] = macc[...] + table_dot(stack_split(waved), t1h[:, cols], t1l[:, cols], True)

    def turn(mask, b, c):
        at = slice(c * piece, (c + 1) * piece)
        for u in range(held):
            flip[mask, b, u * TB : (u + 1) * TB, at] = land[mask, b, u, at, :].T

    density_sends = []

    def send_density(mask):
        if mask:
            copy = remote(
                part.at[mask], part_in.at[mask], dsend.at[mask], drecv.at[mask], dev=me ^ mask
            )
            copy.start()
            density_sends.append(copy)

    rounds = [(None, [0] * batches)]
    for stage in range(bits):
        for low in range(1 << stage):
            masks = []
            for b in range(batches):
                got = 1 << order_of(b)[stage]
                for t in range(stage):
                    if low >> t & 1:
                        got ^= 1 << order_of(b)[t]
                masks.append(got)
            rounds.append((stage, masks))
    done = {}
    for copy in moved:
        copy.wait()
    lax.fori_loop(0, n, tables, 0)
    for number, (stage, masks) in enumerate(rounds):
        last = number == len(rounds) - 1
        for b in range(batches):
            assemble(masks[b], b)
        if last:
            for copy in wave_copies:
                copy.wait()
            far_rows()
            lax.fori_loop(0, n * here // (2 * TB), far_cols, 0)
        for c in range(parts):
            for b in range(batches):
                mask = masks[b]
                if stage is not None:
                    there = landing(mask, b, c)
                    bit = 1 << order_of(b)[stage]
                    remote(
                        there, there, send.at[b, c, mask], recv.at[b, c, mask], dev=me ^ bit
                    ).wait_recv()
                    for later in range(stage + 1, bits):
                        copy = orb_copy(b, later, mask, c)
                        copy.start()
                        started.append(copy)
            sources = [process(masks[b], b, c) for b in range(batches)]
            if not (last and c == parts - 1):
                for source in sources:
                    gather(*source)
            if not last:
                for b in range(batches):
                    turn(masks[b], b, c)
        for mask in masks:
            done[mask] = done.get(mask, 0) + 1
            if done[mask] == batches and not last:
                send_density(mask)

    column = jnp.sum(qacc[...], axis=1, keepdims=True)
    shape = (rows, lanes)
    lane = lax.broadcasted_iota(i32, shape, 1)
    row = lax.broadcasted_iota(i32, shape, 0)
    spot = jnp.where(lane == grp * rows + row, jnp.broadcast_to(column, shape), 0.0)
    mine = jnp.sum(spot, axis=0, keepdims=True)
    charge[0] = mine
    pl.semaphore_wait(ready, n - 1)
    charge_copies = []
    for step in reversed(range(regions)):
        for mask in reversed(range(n)):
            if step or mask:
                slot = step * n + mask
                copy = remote(
                    charge.at[0], charge_in.at[slot], qsend.at[slot], qrecv.at[slot],
                    grp=lax.rem(grp + step, regions), dev=me ^ mask,
                )
                copy.start()
                charge_copies.append(copy)
    for source in sources:
        gather(*source)
    waved = macc[...]
    sums = []
    for z in range(FZ):
        cos = waved[z * rows : (z + 1) * rows]
        sin = waved[(FZ + z) * rows : (FZ + z + 1) * rows]
        sums.append(cos + half_turn(sin, -1.0, 1.0))
        moments[z] = sums[z]
    moment_copies = []
    for mask in range(1, n):
        copy = remote(
            moments, moments_in.at[mask], tsend.at[mask], trecv.at[mask], dev=me ^ mask
        )
        copy.start()
        moment_copies.append(copy)
    for mask in dict.fromkeys(rounds[-1][1]):
        send_density(mask)
    for c in range(parts):
        for b in range(batches):
            turn(rounds[-1][1][b], b, c)
    for copy in moment_copies:
        copy.wait()
    lane, fx, fy = lane_modes((rows, TB))
    first, second = [], []
    for z in range(FZ):
        for mask in range(1, n):
            sums[z] = sums[z] + moments_in[mask, z]
        gain = 0.1 / (1.0 + 0.1 * (fx * fx + fy * fy + float(z * z)))
        value = sums[z] * gain
        first.append(value)
        second.append(half_turn(value, 1.0, -1.0))
    both = stack_split(jnp.concatenate(first + second, axis=0))

    def near_cols(first, count):
        cols = pl.ds(first, count)
        out = table_dot(both, t1h[:, cols], t1l[:, cols], False)
        total = jnp.zeros((rows, count), f32)
        for j in range(WAVES):
            total = total + out[j * rows : (j + 1) * rows] * t2[j : j + 1, cols]
        near_acc[:, cols] = jnp.sum(total * spread[:, cols], axis=0, keepdims=True)

    for q in range(0, n * here, here):
        near_cols(q, here)
    for copy in density_sends:
        copy.wait()
    rho = part[0]
    for mask in range(1, n):
        rho = rho + part_in[mask]
    density[...] = rho
    for copy in started:
        copy.wait_send()

    for copy in charge_copies:
        copy.wait()
    total = mine
    for slot in range(1, n * regions):
        total = total + charge_in[slot]
    every = regions * rows
    shape = (every, lanes)
    lane = lax.broadcasted_iota(i32, shape, 1)
    row = lax.broadcasted_iota(i32, shape, 0)
    spot = jnp.where(lane == row, jnp.broadcast_to(total, shape), 0.0)
    column = jnp.sum(spot, axis=1, keepdims=True)
    for q in range(0, n * here, here):
        cols = slice(q, q + here)
        field = near_acc[:, cols] + jnp.sum(far[:, cols] * column, axis=0, keepdims=True)
        if q == 0:
            potential[...] = field
        scaled[q // here] = wrow[:, cols] * field


def hamilton_kernel(
    union, meta_v, land, flip, scaled, density8, potential8, out, density, potential,
    meta, result, meta_sem, out_sem, *scratch,
):
    n, batches, held, points = land.shape[:4]
    stored = out.shape[0]
    me = lax.axis_index("dev")
    rights, totals = scratch[:batches], scratch[batches:]
    banks = len(totals)
    fetch = pltpu.make_async_copy(meta_v, meta, meta_sem)
    fetch.start()
    for q in range(density.shape[0]):
        density[q : q + 1, :] = density8[0:1, q * TB : (q + 1) * TB]
        potential[q : q + 1, :] = potential8[0:1, q * TB : (q + 1) * TB]

    def clear(t, carry):
        for total in totals:
            total[t] = jnp.zeros((TB, TB), f32)
        return carry

    def prepare(mask, b):
        line = scaled[mask, :, b * points : (b + 1) * points]
        column = jnp.broadcast_to(line, (TB, points)).T
        for j in range(held):
            rights[b][:, j * TB : (j + 1) * TB] = (column * land[mask, b, j].astype(f32)).astype(bf16)

    def one(mask, carry):
        e = me ^ mask
        for b in range(batches):
            if b + 1 < batches:
                prepare(mask, b + 1)
            else:
                prepare(jnp.minimum(mask + 1, n - 1), 0)
            left = flip[mask, b]
            spots = [meta[e, 1 + b, i] for i in range(held)]
            turn = 0
            for j in range(0, held, 2):
                some = min(2, held - j)
                right = rights[b][:, j * TB : (j + some) * TB]
                for first in range(0, held, 2):
                    product = jnp.dot(
                        left[first * TB : (first + 2) * TB], right, preferred_element_type=f32
                    )
                    for i in range(first, min(first + 2, held)):
                        for t in range(some):
                            slot = meta[e, 0, spots[i] * union + spots[j + t]]
                            at = slice((i - first) * TB, (i - first + 1) * TB)
                            tile = product[at, t * TB : (t + 1) * TB]
                            total = totals[turn % banks]
                            total[slot] = total[slot] + tile
                            turn += 1
        return carry

    lax.fori_loop(0, stored + 1, clear, 0)
    prepare(0, 0)
    fetch.wait()
    lax.fori_loop(0, n, one, 0, unroll=4)

    group = math.gcd(stored, 8)
    copies = []
    for first in range(0, stored, group):
        def finish(t, carry):
            value = totals[0][t]
            for total in totals[1:]:
                value = value + total[t]
            result[t] = value.astype(bf16)
            return carry

        lax.fori_loop(first, first + group, finish, 0)
        at = pl.ds(first, group)
        copy = pltpu.make_async_copy(result.at[at], out.at[at], out_sem.at[first // group])
        copy.start()
        copies.append(copy)
    for copy in copies:
        copy.wait()


def on_device(
    n, regions, orbitals, dens_tiles, point_coords, point_weights, batch_blocks,
    tile_owner, tile_slot, batch_atoms, batch_weights, atom_grid_index,
):
    stored = dens_tiles.shape[0]
    listed = tile_slot.shape[0]
    batches, points, width = orbitals.shape
    here = batches * points
    held = width // TB
    atoms = atom_grid_index.shape[1]
    rows = -(-atoms // 8) * 8
    parts = 2
    banks = 2
    table = (-(-(1 + 3 * batches) // 8) * 8, -(-listed // TB) * TB)
    lanes = -(-regions * rows // TB) * TB
    kept = 4 * n * batches * points * width + 64 * n * here + (1 << 20)
    grant = (62 << 20) - kept
    S = jax.ShapeDtypeStruct
    dma = pltpu.SemaphoreType.DMA
    V = pltpu.VMEM
    density, potential, scaled, meta_all, land, flip = pl.pallas_call(
        functools.partial(region_kernel, n, regions, parts),
        out_shape=(
            V((1, here), f32),
            V((1, here), f32),
            V((n, 1, here), f32),
            V((n, *table), i32),
            V((n, batches, held, points, TB), bf16),
            V((n, batches, width, points), bf16),
        ),
        in_specs=[ANY, VM, VM, VM, VM, VM, VM, VM, ANY, SM],
        out_specs=(VM, VM, VM, VM, VM, VM),
        scratch_shapes=[
            V(table, i32),
            V((n, *table), i32),
            pltpu.SMEM((n, *table), i32),
            V((n, 3, here), f32),
            V((n, 1, here), f32),
            V((stored + 1, TB, TB), bf16),
            V((batches, width, width), bf16),
            V((2 * FXY, n * here), bf16),
            V((2 * FXY, n * here), bf16),
            V((WAVES, n * here), f32),
            V((rows, n * here), f32),
            V((1, n * here), f32),
            V((regions * rows, n * here), f32),
            V((1, WAVES * regions * rows, TB), f32),
            V((regions, FZ, rows, TB), f32),
            V((n, 1, here), f32),
            V((n, 1, here), f32),
            V((WAVES * rows, TB), f32),
            V((FZ, rows, TB), f32),
            V((n, FZ, rows, TB), f32),
            V((1, n * here), f32),
            V((rows, TB), f32),
            V((1, 1, lanes), f32),
            V((n * regions, 1, lanes), f32),
            dma((batches, held)),
            dma((4,)),
            dma((batches, parts, n)), dma((batches, parts, n)),
            dma((3, n)), dma((3, n)),
            dma((regions,)), dma((regions,)),
            dma((n,)), dma((n,)), dma((n,)), dma((n,)),
            dma((n * regions,)), dma((n * regions,)),
            pltpu.SemaphoreType.REGULAR,
        ],
        compiler_params=pltpu.CompilerParams(
            collective_id=0, has_side_effects=True, vmem_limit_bytes=grant
        ),
        name="region",
    )(
        orbitals, tile_owner.reshape(1, listed), tile_slot.reshape(1, listed), batch_blocks,
        batch_atoms, batch_weights, point_coords, point_weights.reshape(1, here), dens_tiles,
        atom_grid_index,
    )
    density, potential, scaled, meta_all, land, flip = [
        pltpu.with_memory_space_constraint(value, pltpu.VMEM)
        for value in (density, potential, scaled, meta_all, land, flip)
    ]
    ham_tiles, density, potential = pl.pallas_call(
        functools.partial(hamilton_kernel, math.isqrt(listed)),
        out_shape=(
            S((stored, TB, TB), bf16), S((here // TB, TB), f32), S((here // TB, TB), f32),
        ),
        in_specs=[VM, VM, VM, VM, VM, VM],
        out_specs=(ANY, VM, VM),
        scratch_shapes=[
            pltpu.SMEM((n, *table), i32),
            V((stored, TB, TB), bf16),
            dma,
            dma((stored // math.gcd(stored, 8),)),
            *[V((points, width), bf16) for _ in range(batches)],
            *[V((stored + 1, TB, TB), f32) for _ in range(banks)],
        ],
        compiler_params=pltpu.CompilerParams(vmem_limit_bytes=grant),
        name="hamilton",
    )(meta_all, land, flip, scaled, density, potential)
    return density.reshape(-1), potential.reshape(-1), ham_tiles


def solution(mesh):
    body = functools.partial(on_device, mesh.shape["dev"], mesh.shape["grp"])
    in_specs = (
        P(("grp", "dev"), None, None),
        P(("grp", "dev"), None, None),
        P(None, ("grp", "dev")),
        P(("grp", "dev")),
        P(("grp", "dev"), None),
        P(("grp", "dev"), None),
        P(("grp", "dev")),
        P(("grp", "dev"), None),
        P(("grp", "dev"), None),
        P(None, "grp"),
    )
    out_specs = (P(("grp", "dev")), P(("grp", "dev")), P(("grp", "dev"), None, None))
    return jax.shard_map(body, mesh=mesh, in_specs=in_specs, out_specs=out_specs, check_vma=False)
```
